256 devices in a mesh: gx: 32 (over z_lo, x, core), gz: 8 (over y, z_hi).
Axes of the slice: x: 4, y: 4, z: 8 (z_hi: 2, z_lo: 4; z = z_hi * 4 + z_lo), core: 2. Of those that a mesh axis runs over, the one named last changes fastest.
Arguments:
- u_vel: bfloat16 [512, 384, 768], P('gx', 'gz'), may hold values from -6 to 6
- v_vel: bfloat16 [512, 384, 768], P('gx', 'gz'), may hold values from -6 to 6
- w_vel: bfloat16 [512, 384, 768], P('gx', 'gz'), may hold values from -6 to 6
Outputs:
- pressure: float32 [512, 384, 768], P('gx', 'gz')
- u_new: float32 [512, 384, 768], P('gx', 'gz')
- v_new: float32 [512, 384, 768], P('gx', 'gz')
- w_new: float32 [512, 384, 768], P('gx', 'gz')
The draws below stay inside these ranges and needn't reach their ends.
All inputs are finite; a program needn't handle non-finite values.
Results may differ from the reference program's by a relative error of at most 0.002.
Values may be sent and summed in bfloat16 or wider, within the bound.
A program may use at most 128 MiB of HBM per device.

```python
import math
import jax
import jax.numpy as jnp
from jax import lax

NX = 512
NY = 768
NZ = 384


def level_of(stream_key, dims, shards, smallest, largest):
    level, own = 1.0, jax.random.fold_in(stream_key, 6)
    for axis_at, blocks in shards:
        heights = jnp.exp(jax.random.uniform(jax.random.fold_in(own, axis_at), (blocks,), jnp.float32, smallest / len(shards), largest / len(shards)))
        level = level * jnp.repeat(heights, dims[axis_at] // blocks).reshape([-1 if axis == axis_at else 1 for axis in range(len(dims))])
    return level


def centred(stream_key, extent, scale, most, shards=(), kind=jnp.bfloat16):
    factor_of = level_of(stream_key, extent, shards, -0.22, 0.18) if shards else 1.0
    result = jax.random.normal(stream_key, extent, jnp.float32) * scale * factor_of
    return jnp.minimum(jnp.maximum(result, -most), most).astype(kind)


def setup_inputs(seed: int = 0) -> dict:
    streams_of = jax.random.split(jax.random.key(seed), 4)
    return {
        "u_vel": centred(streams_of[0], (NX, NZ, NY), 1.0, 6.0, ((0, 32), (1, 8))),
        "v_vel": centred(streams_of[1], (NX, NZ, NY), 1.0, 6.0, ((0, 32), (1, 8))),
        "w_vel": centred(streams_of[2], (NX, NZ, NY), 1.0, 6.0, ((0, 32), (1, 8))),
    }


def hartley_table(count):
    index = jnp.arange(count, dtype=jnp.int32)
    product = index[:, None] * index[None, :] % count
    angle = product.astype(jnp.float32) * (2.0 * math.pi / count)
    return jnp.cos(angle) + jnp.sin(angle)

def sine_table(count):
    index = jnp.arange(1, count + 1, dtype=jnp.int32)
    product = index[:, None] * index[None, :] % (2 * (count + 1))
    angle = product.astype(jnp.float32) * (math.pi / (count + 1))
    return math.sqrt(2.0 / (count + 1)) * jnp.sin(angle)

def periodic_eigen(count):
    index = jnp.arange(count, dtype=jnp.int32).astype(jnp.float32)
    return -4.0 * jnp.sin(index * (math.pi / count)) ** 2

def wall_eigen(count):
    index = jnp.arange(1, count + 1, dtype=jnp.int32).astype(jnp.float32)
    return -4.0 * jnp.sin(index * (math.pi / (2 * count + 2))) ** 2

def wall_slope(field):
    padded = jnp.pad(field, ((0, 0), (0, 0), (1, 1)))
    return 0.5 * (padded[:, :, 2:] - padded[:, :, :-2])

def reference(u_vel, v_vel, w_vel):
    hi = lax.Precision.HIGHEST
    uf = u_vel.astype(jnp.float32)
    vf = v_vel.astype(jnp.float32)
    wf = w_vel.astype(jnp.float32)
    div = 0.5 * (jnp.roll(uf, -1, 0) - jnp.roll(uf, 1, 0))
    div = div + 0.5 * (jnp.roll(wf, -1, 1) - jnp.roll(wf, 1, 1))
    div = div + wall_slope(vf)
    sine = sine_table(NY)
    hx = hartley_table(NX)
    hz = hartley_table(NZ)
    spec = jnp.einsum('xzy,ym->xzm', div, sine, precision=hi)
    spec = jnp.einsum('kx,xzm->kzm', hx, spec, precision=hi)
    spec = jnp.einsum('xzm,zq->xqm', spec, hz, precision=hi)
    lam = periodic_eigen(NX)[:, None, None] + periodic_eigen(NZ)[None, :, None] + wall_eigen(NY)[None, None, :]
    spec = spec / (lam * float(NX * NZ))
    spec = jnp.einsum('xqm,zq->xzm', spec, hz, precision=hi)
    spec = jnp.einsum('kx,xzm->kzm', hx, spec, precision=hi)
    pressure = jnp.einsum('xzm,my->xzy', spec, sine, precision=hi)
    slope_x = 0.5 * (jnp.roll(pressure, -1, 0) - jnp.roll(pressure, 1, 0))
    slope_z = 0.5 * (jnp.roll(pressure, -1, 1) - jnp.roll(pressure, 1, 1))
    u_new = uf - slope_x
    v_new = vf - wall_slope(pressure)
    w_new = wf - slope_z
    return (pressure, u_new, v_new, w_new)
```

```python
import math

import jax
import jax.numpy as jnp
from jax import lax
from jax.sharding import PartitionSpec as P

import numpy as np

HI = lax.Precision.HIGH


def hartley_np(count):
    index = np.arange(count)
    angle = (index[:, None] * index[None, :] % count) * (2.0 * np.pi / count)
    return np.cos(angle) + np.sin(angle)


def sine_np(count):
    index = np.arange(1, count + 1)
    angle = (index[:, None] * index[None, :] % (2 * (count + 1))) * (np.pi / (count + 1))
    return np.sqrt(2.0 / (count + 1)) * np.sin(angle)


def wall_eigen_np(count):
    return 4.0 * np.sin(np.arange(1, count + 1) * (np.pi / (2 * count + 2))) ** 2


def periodic_eigen_np(count):
    return 4.0 * np.sin(np.arange(count) * (np.pi / count)) ** 2


def edge_rows(cx, cz):
    grid = np.arange(cx * cz).reshape(cx, cz)
    return np.concatenate([grid[0], grid[-1], grid[:, 0], grid[:, -1]])


def f32(array):
    return jnp.asarray(np.asarray(array, np.float32))


def owner_solve(seen, lam_m, ngx, ngz, cx, cz):
    nx, nz = ngx * cx, ngz * cz
    per = seen.shape[1]
    hx = hartley_np(nx)
    hz = hartley_np(nz)
    block_x = np.arange(ngx) * cx
    block_z = np.arange(ngz) * cz
    line_x = np.concatenate([(block_x - 1) % nx, (block_x + cx) % nx])
    line_z = np.concatenate([(block_z - 1) % nz, (block_z + cz) % nz])
    lx = f32(hx[:, line_x])
    lz = f32(hz[:, line_z])
    hx, hz = f32(hx), f32(hz)
    five = seen.reshape(ngx, ngz, per, -1)
    sx = five[..., : 2 * cz].reshape(ngx, ngz, per, 2, cz)
    sz = five[..., 2 * cz :].reshape(ngx, ngz, per, 2, cx)
    px = sx.transpose(2, 3, 0, 1, 4).reshape(per, 2 * ngx, nz)
    pz = sz.transpose(2, 3, 1, 0, 4).reshape(per, 2 * ngz, nx)
    f1 = jnp.einsum("mlz,zk->mlk", px, hz, precision=HI)
    f2 = jnp.einsum("mlx,xk->mlk", pz, hx, precision=HI)
    spec = jnp.einsum("kl,mlq->mkq", lx, f1, precision=HI) + jnp.einsum(
        "mlk,ql->mkq", f2, lz, precision=HI
    )
    lam = (
        f32(periodic_eigen_np(nx))[None, :, None]
        + f32(periodic_eigen_np(nz))[None, None, :]
        + lam_m[:, None, None]
    )
    spec = spec / (lam * float(nx * nz))
    ex = jnp.einsum("kl,mkq->mlq", lx, spec, precision=HI)
    ex = jnp.einsum("mlq,zq->mlz", ex, hz, precision=HI)
    ez = jnp.einsum("ql,mkq->mlk", lz, spec, precision=HI)
    ez = jnp.einsum("mlk,xk->mlx", ez, hx, precision=HI)
    px = px.reshape(per, 2, ngx, nz)
    pz = pz.reshape(per, 2, ngz, nx)
    swap_x = jnp.stack([jnp.roll(px[:, 1], 1, 1), jnp.roll(px[:, 0], -1, 1)], 1)
    swap_z = jnp.stack([jnp.roll(pz[:, 1], 1, 1), jnp.roll(pz[:, 0], -1, 1)], 1)
    tx = ex.reshape(per, 2, ngx, ngz, cz) + swap_x.reshape(per, 2, ngx, ngz, cz)
    tz = ez.reshape(per, 2, ngz, ngx, cx) + swap_z.reshape(per, 2, ngz, ngx, cx)
    tx = tx.transpose(2, 3, 0, 1, 4).reshape(ngx, ngz, per, 2 * cz)
    tz = tz.transpose(3, 2, 0, 1, 4).reshape(ngx, ngz, per, 2 * cx)
    return jnp.concatenate([tx, tz], -1).reshape(ngx * ngz, per, 2 * (cx + cz))


def shifted(block, axis, step):
    count = lax.axis_size(axis)
    return lax.ppermute(block, axis, [(i, (i + step) % count) for i in range(count)])


def on_device(u_vel, v_vel, w_vel):
    cx, cz, ny = u_vel.shape
    ngx = lax.axis_size("gx")
    ngz = lax.axis_size("gz")
    devices = ngx * ngz
    per = ny // devices
    me = lax.axis_index("gx") * ngz + lax.axis_index("gz")
    u_low = shifted(u_vel[-1:], "gx", 1).astype(jnp.float32)
    u_high = shifted(u_vel[:1], "gx", -1).astype(jnp.float32)
    w_low = shifted(w_vel[:, -1:], "gz", 1).astype(jnp.float32)
    w_high = shifted(w_vel[:, :1], "gz", -1).astype(jnp.float32)
    uf = u_vel.astype(jnp.float32)
    vf = v_vel.astype(jnp.float32)
    wf = w_vel.astype(jnp.float32)
    up = jnp.pad(uf, ((1, 1), (0, 0), (0, 0)))
    vp = jnp.pad(vf, ((0, 0), (0, 0), (1, 1)))
    wp = jnp.pad(wf, ((0, 0), (1, 1), (0, 0)))
    div = 0.5 * ((up[2:] - up[:-2]) + (vp[:, :, 2:] - vp[:, :, :-2]) + (wp[:, 2:] - wp[:, :-2]))
    rim = jnp.concatenate([-0.5 * uf[0], 0.5 * uf[-1], -0.5 * wf[:, 0], 0.5 * wf[:, -1]], 0)
    sine = f32(sine_np(ny))
    local = np.kron(sine_np(cx), sine_np(cz))
    edge = f32(local[edge_rows(cx, cz)])
    local = f32(local)
    mu = f32(np.add.outer(wall_eigen_np(cx), wall_eigen_np(cz)).reshape(-1))[:, None] + f32(
        wall_eigen_np(ny)
    )
    wide = jnp.dot(jnp.concatenate([div.reshape(cx * cz, ny), rim], 0), sine, precision=HI)
    modes = jnp.dot(local, wide[: cx * cz], precision=HI)
    q_edge = jnp.dot(edge, modes / mu, precision=HI)
    send = (wide[cx * cz :] - q_edge).T.reshape(devices, per, -1)
    seen = lax.all_to_all(send, ("gx", "gz"), split_axis=0, concat_axis=0, tiled=True)
    lam_m = lax.dynamic_slice(f32(wall_eigen_np(ny)), (me * per,), (per,))
    back = owner_solve(seen, lam_m, ngx, ngz, cx, cz)
    got = lax.all_to_all(back, ("gx", "gz"), split_axis=0, concat_axis=0, tiled=True)
    ring = got.reshape(ny, -1).T
    field = (jnp.dot(edge.T, ring, precision=HI) - modes) / mu
    field = jnp.dot(local, field, precision=HI)
    wide = jnp.dot(jnp.concatenate([field, ring], 0), sine, precision=HI)
    pressure = wide[: cx * cz].reshape(cx, cz, ny)
    ring = wide[cx * cz :]
    p_low = ring[None, :cz] - 0.5 * u_low
    p_high = ring[None, cz : 2 * cz] + 0.5 * u_high
    pz_low = ring[2 * cz : 2 * cz + cx][:, None] - 0.5 * w_low
    pz_high = ring[2 * cz + cx :][:, None] + 0.5 * w_high
    px = jnp.concatenate([p_low, pressure, p_high], 0)
    pz = jnp.concatenate([pz_low, pressure, pz_high], 1)
    py = jnp.pad(pressure, ((0, 0), (0, 0), (1, 1)))
    u_new = uf - 0.5 * (px[2:] - px[:-2])
    v_new = vf - 0.5 * (py[:, :, 2:] - py[:, :, :-2])
    w_new = wf - 0.5 * (pz[:, 2:] - pz[:, :-2])
    return (pressure, u_new, v_new, w_new)


def solution(mesh):
    spec = P("gx", "gz", None)
    return jax.shard_map(
        on_device, mesh=mesh, in_specs=(spec,) * 3, out_specs=(spec,) * 4, check_vma=False
    )
```

```python
import functools
import math

import jax
import jax.numpy as jnp
import numpy as np
from jax import lax
from jax.experimental import pallas as pl
from jax.experimental.pallas import tpu as pltpu
from jax.sharding import PartitionSpec as P

F32 = jnp.float32
BF16 = jnp.bfloat16
TILE = 256
LANES = 128


def hartley_np(count):
    index = np.arange(count)
    angle = (index[:, None] * index[None, :] % count) * (2.0 * np.pi / count)
    return np.cos(angle) + np.sin(angle)


def sine_np(count):
    index = np.arange(1, count + 1)
    angle = (index[:, None] * index[None, :] % (2 * (count + 1))) * (np.pi / (count + 1))
    return np.sqrt(2.0 / (count + 1)) * np.sin(angle)


def sine_parts_np(count, step):
    mode = np.arange(1, count + 1)
    coarse = np.arange(0, count, step)
    fine = np.arange(1, step + 1)
    size = np.sqrt(2.0 / (count + 1))
    angle_c = (coarse[:, None] * mode % (2 * (count + 1))) * (np.pi / (count + 1))
    angle_f = (fine[:, None] * mode % (2 * (count + 1))) * (np.pi / (count + 1))
    return (
        size * np.sin(angle_c),
        size * np.cos(angle_c),
        np.sin(angle_f),
        np.cos(angle_f),
    )


def wall_eigen_np(count):
    return 4.0 * np.sin(np.arange(1, count + 1) * (np.pi / (2 * count + 2))) ** 2


def periodic_eigen_np(count):
    return 4.0 * np.sin(np.arange(count) * (np.pi / count)) ** 2


def edge_rows(cx, cz):
    grid = np.arange(cx * cz).reshape(cx, cz)
    return np.concatenate([grid[0], grid[-1], grid[:, 0], grid[:, -1]])


def f32(array):
    return np.ascontiguousarray(np.asarray(array, np.float32))


def halves(array):
    array = np.asarray(array, np.float32)
    high = array.astype(BF16)
    low = (array - high.astype(np.float32)).astype(BF16)
    return [high, low]


def split(x):
    high = x.astype(BF16)
    return high, (x - high.astype(F32)).astype(BF16)


def dot(a, b):
    return jnp.dot(a, b, preferred_element_type=F32)


def dot_t(a, b):
    return lax.dot_general(a, b, (((1,), (1,)), ((), ())), preferred_element_type=F32)


def dot3(a, b, op=dot):
    return op(a[0], b[0]) + op(a[1], b[0]) + op(a[0], b[1])


def fill_sine(parts, high, low):
    sa, ca, sb, cb = parts
    step = sb.shape[0]

    @pl.loop(0, sa.shape[0])
    def _(a):
        block = sa[pl.ds(a, 1), :] * cb[...] + ca[pl.ds(a, 1), :] * sb[...]
        rows = pl.ds(pl.multiple_of(a * step, step), step)
        high[rows, :], low[rows, :] = split(block)


def fill_local(sx, sz, high, low):
    step = sz.shape[0]

    @pl.loop(0, sx.shape[0])
    def _(a):
        rows = pl.ds(pl.multiple_of(a * step, step), step)
        high[rows, :], low[rows, :] = split(sx[pl.ds(a, 1), :] * sz[...])


def along_rows(x, first, last):
    rows = x.shape[0]
    at = lax.broadcasted_iota(jnp.int32, x.shape, 0)
    up = jnp.where(at == rows - 1, last, pltpu.roll(x, rows - 1, 0))
    down = jnp.where(at == 0, first, pltpu.roll(x, 1, 0))
    return up - down


def along_lanes(x):
    lanes = x.shape[1]
    at = lax.broadcasted_iota(jnp.int32, x.shape, 1)
    up = jnp.where(at == lanes - 1, 0.0, pltpu.roll(x, lanes - 1, 1))
    down = jnp.where(at == 0, 0.0, pltpu.roll(x, 1, 1))
    return up - down


def forward_kernel(
    u, v, w, sa, ca, sb, cb, sx, sz, eh, el, mux, mum, send, modes, sh, sl, kh, kl, dh, dl
):
    cx, cz, ny = u.shape
    cells = cx * cz
    fill_sine((sa, ca, sb, cb), sh, sl)
    fill_local(sx, sz, kh, kl)

    @pl.loop(0, cx)
    def _(x):
        after = u[jnp.minimum(x + 1, cx - 1)].astype(F32) * jnp.where(x < cx - 1, 1.0, 0.0)
        before = u[jnp.maximum(x - 1, 0)].astype(F32) * jnp.where(x > 0, 1.0, 0.0)
        div = 0.5 * (
            (after - before)
            + along_lanes(v[x].astype(F32))
            + along_rows(w[x].astype(F32), 0.0, 0.0)
        )
        rows = pl.ds(pl.multiple_of(x * cz, cz), cz)
        dh[rows, :], dl[rows, :] = split(div)

    dh[cells : cells + cz, :] = (-0.5 * u[0].astype(F32)).astype(BF16)
    dh[cells + cz : cells + 2 * cz, :] = (0.5 * u[cx - 1].astype(F32)).astype(BF16)
    dh[cells + 2 * cz : cells + 2 * cz + cx, :] = (-0.5 * w[:, 0, :].astype(F32)).astype(BF16)
    dh[cells + 2 * cz + cx :, :] = (0.5 * w[:, cz - 1, :].astype(F32)).astype(BF16)

    @pl.loop(0, ny // TILE)
    def _(n):
        cols = pl.ds(pl.multiple_of(n * TILE, TILE), TILE)
        wide = dot(dh[...], sh[:, cols]) + dot(dh[...], sl[:, cols])
        field = wide[:cells] + dot(dl[...], sh[:, cols])
        mode = dot3((kh[...], kl[...]), split(field))
        modes[:, cols] = mode
        mode = mode / (mux[...] + mum[:, cols])
        edge = wide[cells:] - dot3((eh[...], el[...]), split(mode))
        send[cols, :] = edge.T


def owner_kernel(
    ngx, ngz, cx, cz, seen, hxh, hxl, hzh, hzl, lxh, lxl, lxth, lxtl, lzth, lztl, muz, mukx, mum, out
):
    per = mum.shape[0]
    nx, nz = ngx * cx, ngz * cz
    lane = lax.broadcasted_iota(jnp.int32, (ngx, LANES), 1)
    lane8 = lax.broadcasted_iota(jnp.int32, (ngz, LANES), 1)
    wide_x = nz // LANES
    wide_z = nx // LANES
    hx = (hxh[...], hxl[...])
    hz = (hzh[...], hzl[...])
    px, pz = [], []
    for m in range(per):
        cols = [[jnp.zeros((ngx, LANES), F32)] * wide_x for _ in range(2)]
        for j in range(ngz):
            piece = seen[pl.ds(j * per + m, ngx, stride=ngz * per), :]
            for f in range(2):
                turned = pltpu.roll(piece, (cz * j - cz * f) % LANES, 1)
                for c in range(wide_x):
                    low, high = cz * j - c * LANES, cz * (j + 1) - c * LANES
                    if high > 0 and low < LANES:
                        cols[f][c] = jnp.where((lane >= low) & (lane < high), turned, cols[f][c])
        px += [jnp.concatenate(c, 1) for c in cols]
        cols = [[jnp.zeros((ngz, LANES), F32)] * wide_z for _ in range(2)]
        for i in range(ngx):
            piece = seen[pl.ds(i * ngz * per + m, ngz, stride=per), :]
            c, low = cx * i // LANES, cx * i % LANES
            for f in range(2):
                turned = pltpu.roll(piece, (low - 2 * cz - cx * f) % LANES, 1)
                cols[f][c] = jnp.where((lane8 >= low) & (lane8 < low + cx), turned, cols[f][c])
        pz += [jnp.concatenate(c, 1) for c in cols]
    f1 = dot3(split(jnp.concatenate(px, 0)), hz)
    f2 = dot3(split(jnp.concatenate(pz, 0)), hx)
    ex, ez = [], []
    for m in range(per):
        mine = f1[2 * ngx * m : 2 * ngx * (m + 1)]
        other = f2[2 * ngz * m : 2 * ngz * (m + 1)].T
        spec = dot3((lxh[...], lxl[...]), split(mine)) + dot3(split(other), (lzth[...], lztl[...]))
        spec = spec / ((mukx[...] + muz[...] + mum[m : m + 1, :1]) * (-float(nx * nz)))
        spec = split(spec)
        ex.append(dot3((lxth[...], lxtl[...]), spec))
        ez.append(dot3((lzth[...], lztl[...]), spec, dot_t))
    ex = -dot3(split(jnp.concatenate(ex, 0)), hz)
    ez = -dot3(split(jnp.concatenate(ez, 0)), hx)
    for m in range(per):
        tx, tz = [], []
        for f in range(2):
            at = 2 * ngx * m + f * ngx
            turn = 1 if f == 0 else ngx - 1
            tx.append(ex[at : at + ngx] + pltpu.roll(px[2 * m + 1 - f], turn, 0))
            at = 2 * ngz * m + f * ngz
            turn = 1 if f == 0 else ngz - 1
            tz.append(ez[at : at + ngz] + pltpu.roll(pz[2 * m + 1 - f], turn, 0))
        for j in range(ngz):
            c, low = cz * j // LANES, cz * j % LANES
            total = jnp.zeros((ngx, LANES), F32)
            for f in range(2):
                piece = tx[f][:, c * LANES : (c + 1) * LANES]
                if low + cz > LANES:
                    after = tx[f][:, (c + 1) * LANES : (c + 2) * LANES]
                    piece = jnp.where(lane >= low, piece, after)
                piece = pltpu.roll(piece, (cz * f - low) % LANES, 1)
                total = jnp.where((lane >= cz * f) & (lane < cz * (f + 1)), piece, total)
            out[pl.ds(j * per + m, ngx, stride=ngz * per), :] = total
        for i in range(ngx):
            c, low = cx * i // LANES, cx * i % LANES
            rows = pl.ds(i * ngz * per + m, ngz, stride=per)
            total = out[rows, :]
            for f in range(2):
                start = 2 * cz + cx * f
                piece = pltpu.roll(tz[f][:, c * LANES : (c + 1) * LANES], (start - low) % LANES, 1)
                total = jnp.where((lane8 >= start) & (lane8 < start + cx), piece, total)
            out[rows, :] = total


def backward_kernel(
    u, v, w, ul, uh, wl, wh, got, modes, sa, ca, sb, cb, sx, sz, eth, etl, mux, mum,
    pressure, u_new, v_new, w_new, sh, sl, kh, kl, fh, fl, ring, plow, phigh,
):
    cx, cz, ny = u.shape
    cells = cx * cz
    fill_sine((sa, ca, sb, cb), sh, sl)
    fill_local(sx, sz, kh, kl)

    @pl.loop(0, ny // TILE)
    def _(n):
        cols = pl.ds(pl.multiple_of(n * TILE, TILE), TILE)
        edge = split(got[cols, :].T)
        field = dot3((eth[...], etl[...]), edge) - modes[:, cols]
        field = split(field / (mux[...] + mum[:, cols]))
        field = split(dot3((kh[...], kl[...]), field))
        fh[:cells, cols], fl[:cells, cols] = field
        fh[cells:, cols], fl[cells:, cols] = edge

    @pl.loop(0, ny // TILE)
    def _(n):
        cols = pl.ds(pl.multiple_of(n * TILE, TILE), TILE)
        wide = dot3((fh[...], fl[...]), (sh[:, cols], sl[:, cols]))
        pressure[:, :, cols] = wide[:cells].reshape(cx, cz, TILE)
        ring[:, cols] = wide[cells:]

    plow[...] = ring[:cz, :] - 0.5 * ul[...].astype(F32)
    phigh[...] = ring[cz : 2 * cz, :] + 0.5 * uh[...].astype(F32)
    edge = pl.ds(2 * cz, cx)
    ring[edge, :] = ring[edge, :] - 0.5 * wl[...].astype(F32)
    edge = pl.ds(2 * cz + cx, cx)
    ring[edge, :] = ring[edge, :] + 0.5 * wh[...].astype(F32)

    def finish(x, before, after):
        here = pressure[x]
        u_new[x] = u[x].astype(F32) - 0.5 * (after - before)
        v_new[x] = v[x].astype(F32) - 0.5 * along_lanes(here)
        first = ring[pl.ds(2 * cz + x, 1), :]
        last = ring[pl.ds(2 * cz + cx + x, 1), :]
        w_new[x] = w[x].astype(F32) - 0.5 * along_rows(here, first, last)

    finish(0, plow[...], pressure[1])
    finish(cx - 1, pressure[cx - 2], phigh[...])

    @pl.loop(1, cx - 1)
    def _(x):
        finish(x, pressure[x - 1], pressure[x + 1])


def shifted(block, axis, step):
    count = lax.axis_size(axis)
    return lax.ppermute(block, axis, [(i, (i + step) % count) for i in range(count)])


def call(kernel, name, outs, scratch, flops, *args):
    size = sum(math.prod(a.shape) * a.dtype.itemsize for a in [*args, *outs])
    return pl.pallas_call(
        kernel,
        out_shape=outs,
        in_specs=[pl.BlockSpec(memory_space=pltpu.VMEM)] * len(args),
        out_specs=[pl.BlockSpec(memory_space=pltpu.VMEM)] * len(outs),
        scratch_shapes=scratch,
        compiler_params=pltpu.CompilerParams(vmem_limit_bytes=60 << 20),
        cost_estimate=pl.CostEstimate(flops=flops, bytes_accessed=size, transcendentals=0),
        name=name,
    )(*args)


def on_device(u_vel, v_vel, w_vel):
    cx, cz, ny = u_vel.shape
    ngx = lax.axis_size("gx")
    ngz = lax.axis_size("gz")
    nx, nz = ngx * cx, ngz * cz
    devices = ngx * ngz
    per = ny // devices
    cells = cx * cz
    edges = 2 * (cx + cz)
    me = lax.axis_index("gx") * ngz + lax.axis_index("gz")
    u_low = shifted(u_vel[-1], "gx", 1)
    u_high = shifted(u_vel[0], "gx", -1)
    w_low = shifted(w_vel[:, -1], "gz", 1)
    w_high = shifted(w_vel[:, 0], "gz", -1)
    local = np.kron(sine_np(cx), sine_np(cz))[edge_rows(cx, cz)]
    tables = [f32(t) for t in sine_parts_np(ny, 32)]
    tables += [f32(np.repeat(sine_np(cx), cz, 1)), f32(np.tile(sine_np(cz), (1, cx)))]
    mux = f32(np.add.outer(wall_eigen_np(cx), wall_eigen_np(cz)).reshape(-1, 1))
    mum = f32(wall_eigen_np(ny).reshape(1, -1))
    shape = jax.ShapeDtypeStruct
    square = [pltpu.VMEM((ny, ny), BF16)] * 2 + [pltpu.VMEM((cells, cells), BF16)] * 2
    send, modes = call(
        forward_kernel,
        "forward",
        [shape((ny, edges), F32), shape((cells, ny), F32)],
        square + [pltpu.VMEM((cells + edges, ny), BF16), pltpu.VMEM((cells, ny), BF16)],
        6 * cells * ny * (ny + cells + edges),
        u_vel, v_vel, w_vel, *tables, *halves(local), mux, mum,
    )
    send = send.reshape(devices, per, 1, edges)
    seen = lax.all_to_all(send, ("gx", "gz"), split_axis=0, concat_axis=0, tiled=True)
    hx, hz = hartley_np(nx), hartley_np(nz)
    block_x, block_z = np.arange(ngx) * cx, np.arange(ngz) * cz
    lx = hx[:, np.concatenate([(block_x - 1) % nx, (block_x + cx) % nx])]
    lz = hz[:, np.concatenate([(block_z - 1) % nz, (block_z + cz) % nz])]
    lam_m = lax.dynamic_slice(jnp.asarray(mum[0]), (me * per,), (per,))
    (back,) = call(
        functools.partial(owner_kernel, ngx, ngz, cx, cz),
        "owner",
        [shape((ny, edges), F32)],
        [],
        6 * per * nx * nz * 200,
        seen.reshape(ny, edges),
        *halves(hx), *halves(hz), *halves(lx), *halves(lx.T), *halves(lz.T),
        f32(periodic_eigen_np(nz).reshape(1, -1)),
        f32(periodic_eigen_np(nx).reshape(-1, 1)),
        jnp.broadcast_to(lam_m[:, None], (per, LANES)),
    )
    back = back.reshape(devices, per, 1, edges)
    got = lax.all_to_all(back, ("gx", "gz"), split_axis=0, concat_axis=0, tiled=True)
    block = shape((cx, cz, ny), F32)
    return tuple(
        call(
            backward_kernel,
            "backward",
            [block] * 4,
            square
            + [pltpu.VMEM((cells + edges, ny), BF16)] * 2
            + [pltpu.VMEM((edges, ny), F32)]
            + [pltpu.VMEM((cz, ny), F32)] * 2,
            6 * cells * ny * (ny + cells + edges),
            u_vel, v_vel, w_vel, u_low, u_high, w_low, w_high, got.reshape(ny, edges), modes,
            *tables, *halves(local.T), mux, mum,
        )
    )


def solution(mesh):
    spec = P("gx", "gz", None)
    return jax.shard_map(
        on_device, mesh=mesh, in_specs=(spec,) * 3, out_specs=(spec,) * 4, check_vma=False
    )
```

```python
import functools
import math

import jax
import jax.numpy as jnp
import numpy as np
from jax import lax
from jax.experimental import pallas as pl
from jax.experimental.pallas import tpu as pltpu
from jax.sharding import PartitionSpec as P

F32 = jnp.float32
BF16 = jnp.bfloat16
TILE = 256
STRIDE = 37
LANES = 128


def hartley_np(count):
    index = np.arange(count)
    angle = (index[:, None] * index[None, :] % count) * (2.0 * np.pi / count)
    return np.cos(angle) + np.sin(angle)


def sine_np(count):
    index = np.arange(1, count + 1)
    angle = (index[:, None] * index[None, :] % (2 * (count + 1))) * (np.pi / (count + 1))
    return np.sqrt(2.0 / (count + 1)) * np.sin(angle)


def sine_parts_np(count, step):
    mode = np.arange(1, count + 1)
    coarse = np.arange(0, count, step)
    fine = np.arange(1, step + 1)
    size = np.sqrt(2.0 / (count + 1))
    angle_c = (coarse[:, None] * mode % (2 * (count + 1))) * (np.pi / (count + 1))
    angle_f = (fine[:, None] * mode % (2 * (count + 1))) * (np.pi / (count + 1))
    return (
        size * np.sin(angle_c),
        size * np.cos(angle_c),
        np.sin(angle_f),
        np.cos(angle_f),
    )


def wall_eigen_np(count):
    return 4.0 * np.sin(np.arange(1, count + 1) * (np.pi / (2 * count + 2))) ** 2


def periodic_eigen_np(count):
    return 4.0 * np.sin(np.arange(count) * (np.pi / count)) ** 2


def edge_rows(cx, cz):
    grid = np.arange(cx * cz).reshape(cx, cz)
    return np.concatenate([grid[0], grid[-1], grid[:, 0], grid[:, -1]])


def f32(array):
    return np.ascontiguousarray(np.asarray(array, np.float32))


def halves(array):
    array = np.asarray(array, np.float32)
    high = array.astype(BF16)
    low = (array - high.astype(np.float32)).astype(BF16)
    return [high, low]


def split(x):
    high = x.astype(BF16)
    return high, (x - high.astype(F32)).astype(BF16)


def dot(a, b):
    return jnp.dot(a, b, preferred_element_type=F32)


def dot_t(a, b):
    return lax.dot_general(a, b, (((1,), (1,)), ((), ())), preferred_element_type=F32)


def dot3(a, b, op=dot):
    return op(a[0], b[0]) + op(a[1], b[0]) + op(a[0], b[1])


def fill_sine(parts, high, low):
    sa, ca, sb, cb = parts
    step = sb.shape[0]

    @pl.loop(0, sa.shape[0])
    def _(a):
        block = sa[pl.ds(a, 1), :] * cb[...] + ca[pl.ds(a, 1), :] * sb[...]
        rows = pl.ds(pl.multiple_of(a * step, step), step)
        high[rows, :], low[rows, :] = split(block)


def fill_local(sx, sz, high, low):
    step = sz.shape[0]

    @pl.loop(0, sx.shape[0])
    def _(a):
        rows = pl.ds(pl.multiple_of(a * step, step), step)
        high[rows, :], low[rows, :] = split(sx[pl.ds(a, 1), :] * sz[...])


def along_rows(x, first, last):
    rows = x.shape[0]
    at = lax.broadcasted_iota(jnp.int32, x.shape, 0)
    up = jnp.where(at == rows - 1, last, pltpu.roll(x, rows - 1, 0))
    down = jnp.where(at == 0, first, pltpu.roll(x, 1, 0))
    return up - down


def along_lanes(x):
    lanes = x.shape[1]
    at = lax.broadcasted_iota(jnp.int32, x.shape, 1)
    up = jnp.where(at == lanes - 1, 0.0, pltpu.roll(x, lanes - 1, 1))
    down = jnp.where(at == 0, 0.0, pltpu.roll(x, 1, 1))
    return up - down


def forward_kernel(
    u, v, w, sa, ca, sb, cb, sx, sz, eh, el, mux, mum, send, modes, wlow, whigh,
    sh, sl, kh, kl, dh, dl
):
    cx, cz, ny = u.shape
    cells = cx * cz
    wlow[...] = w[:, 0, :]
    whigh[...] = w[:, cz - 1, :]
    fill_sine((sa, ca, sb, cb), sh, sl)
    fill_local(sx, sz, kh, kl)

    @pl.loop(0, cx)
    def _(x):
        after = u[jnp.minimum(x + 1, cx - 1)].astype(F32) * jnp.where(x < cx - 1, 1.0, 0.0)
        before = u[jnp.maximum(x - 1, 0)].astype(F32) * jnp.where(x > 0, 1.0, 0.0)
        div = 0.5 * (
            (after - before)
            + along_lanes(v[x].astype(F32))
            + along_rows(w[x].astype(F32), 0.0, 0.0)
        )
        rows = pl.ds(pl.multiple_of(x * cz, cz), cz)
        dh[rows, :], dl[rows, :] = split(div)

    dh[cells : cells + cz, :] = (-0.5 * u[0].astype(F32)).astype(BF16)
    dh[cells + cz : cells + 2 * cz, :] = (0.5 * u[cx - 1].astype(F32)).astype(BF16)
    dh[cells + 2 * cz : cells + 2 * cz + cx, :] = (-0.5 * w[:, 0, :].astype(F32)).astype(BF16)
    dh[cells + 2 * cz + cx :, :] = (0.5 * w[:, cz - 1, :].astype(F32)).astype(BF16)

    @pl.loop(0, ny // TILE)
    def _(n):
        cols = pl.ds(pl.multiple_of(n * TILE, TILE), TILE)
        wide = dot(dh[...], sh[:, cols]) + dot(dh[...], sl[:, cols])
        field = wide[:cells] + dot(dl[...], sh[:, cols])
        mode = dot3((kh[...], kl[...]), split(field))
        modes[:, cols] = mode
        mode = mode / (mux[...] + mum[:, cols])
        edge = wide[cells:] - dot3((eh[...], el[...]), split(mode))
        send[cols, :] = edge.T


def send_blocks(source, target, send_sem, recv_sem, own_sem):
    ngx, ngz = lax.axis_size("gx"), lax.axis_size("gz")
    devices = ngx * ngz
    per = source.shape[0] // devices
    me = lax.axis_index("gx") * ngz + lax.axis_index("gz")
    mine = pl.ds(me * per, per)

    def copy(other):
        return pltpu.make_async_remote_copy(
            src_ref=source.at[pl.ds(other * per, per)],
            dst_ref=target.at[mine],
            send_sem=send_sem,
            recv_sem=recv_sem,
            device_id=(other // ngz, other % ngz),
            device_id_type=pl.DeviceIdType.MESH,
        )

    def start(k, carry):
        copy((me + STRIDE * k) % devices).start()
        return carry

    lax.fori_loop(1, devices, start, 0)
    own = pltpu.make_async_copy(source.at[mine], target.at[mine], own_sem)
    own.start()
    rest = pl.ds(0, (devices - 1) * per)
    everything = pltpu.make_async_remote_copy(
        src_ref=source.at[rest],
        dst_ref=target.at[rest],
        send_sem=send_sem,
        recv_sem=recv_sem,
        device_id=(lax.axis_index("gx"), (lax.axis_index("gz") + 1) % ngz),
        device_id_type=pl.DeviceIdType.MESH,
    )
    return own, everything


def exchange_kernel(source, target, send_sem, recv_sem, own_sem):
    own, everything = send_blocks(source, target, send_sem, recv_sem, own_sem)
    own.wait()
    everything.wait_send()
    everything.wait_recv()


def exchange_halo_kernel(
    source, u, wlow, whigh, target, ul, uh, wl, wh, send_sem, recv_sem, own_sem, hs, hr
):
    ngx, ngz = lax.axis_size("gx"), lax.axis_size("gz")
    gx, gz = lax.axis_index("gx"), lax.axis_index("gz")
    last = u.shape[0] - 1
    plan = [
        (u.at[last], ul, ((gx + 1) % ngx, gz)),
        (u.at[0], uh, ((gx + ngx - 1) % ngx, gz)),
        (whigh, wl, (gx, (gz + 1) % ngz)),
        (wlow, wh, (gx, (gz + ngz - 1) % ngz)),
    ]
    copies = [
        pltpu.make_async_remote_copy(
            src_ref=a,
            dst_ref=b,
            send_sem=hs.at[i],
            recv_sem=hr.at[i],
            device_id=to,
            device_id_type=pl.DeviceIdType.MESH,
        )
        for i, (a, b, to) in enumerate(plan)
    ]
    own, everything = send_blocks(source, target, send_sem, recv_sem, own_sem)
    for c in copies:
        c.start()
    own.wait()
    everything.wait_send()
    everything.wait_recv()
    for c in copies:
        c.wait()


def owner_kernel(
    ngx, ngz, cx, cz, seen, hxh, hxl, hzh, hzl, lxh, lxl, lxth, lxtl, lzth, lztl, muz, mukx, mum, out
):
    per = mum.shape[0] // (ngx * ngz)
    me = lax.axis_index("gx") * ngz + lax.axis_index("gz")
    nx, nz = ngx * cx, ngz * cz
    lane = lax.broadcasted_iota(jnp.int32, (ngx, LANES), 1)
    lane8 = lax.broadcasted_iota(jnp.int32, (ngz, LANES), 1)
    wide_x = nz // LANES
    wide_z = nx // LANES
    hx = (hxh[...], hxl[...])
    hz = (hzh[...], hzl[...])
    px, pz = [], []
    for m in range(per):
        cols = [[jnp.zeros((ngx, LANES), F32)] * wide_x for _ in range(2)]
        for j in range(ngz):
            piece = seen[pl.ds(j * per + m, ngx, stride=ngz * per), :]
            for f in range(2):
                turned = pltpu.roll(piece, (cz * j - cz * f) % LANES, 1)
                for c in range(wide_x):
                    low, high = cz * j - c * LANES, cz * (j + 1) - c * LANES
                    if high > 0 and low < LANES:
                        cols[f][c] = jnp.where((lane >= low) & (lane < high), turned, cols[f][c])
        px += [jnp.concatenate(c, 1) for c in cols]
        cols = [[jnp.zeros((ngz, LANES), F32)] * wide_z for _ in range(2)]
        for i in range(ngx):
            piece = seen[pl.ds(i * ngz * per + m, ngz, stride=per), :]
            c, low = cx * i // LANES, cx * i % LANES
            for f in range(2):
                turned = pltpu.roll(piece, (low - 2 * cz - cx * f) % LANES, 1)
                cols[f][c] = jnp.where((lane8 >= low) & (lane8 < low + cx), turned, cols[f][c])
        pz += [jnp.concatenate(c, 1) for c in cols]
    f1 = dot3(split(jnp.concatenate(px, 0)), hz)
    f2 = dot3(split(jnp.concatenate(pz, 0)), hx)
    ex, ez = [], []
    for m in range(per):
        mine = f1[2 * ngx * m : 2 * ngx * (m + 1)]
        other = f2[2 * ngz * m : 2 * ngz * (m + 1)].T
        spec = dot3((lxh[...], lxl[...]), split(mine)) + dot3(split(other), (lzth[...], lztl[...]))
        spec = spec / ((mukx[...] + muz[...] + mum[me * per + m]) * (-float(nx * nz)))
        spec = split(spec)
        ex.append(dot3((lxth[...], lxtl[...]), spec))
        ez.append(dot3((lzth[...], lztl[...]), spec, dot_t))
    ex = -dot3(split(jnp.concatenate(ex, 0)), hz)
    ez = -dot3(split(jnp.concatenate(ez, 0)), hx)
    for m in range(per):
        tx, tz = [], []
        for f in range(2):
            at = 2 * ngx * m + f * ngx
            turn = 1 if f == 0 else ngx - 1
            tx.append(ex[at : at + ngx] + pltpu.roll(px[2 * m + 1 - f], turn, 0))
            at = 2 * ngz * m + f * ngz
            turn = 1 if f == 0 else ngz - 1
            tz.append(ez[at : at + ngz] + pltpu.roll(pz[2 * m + 1 - f], turn, 0))
        for j in range(ngz):
            c, low = cz * j // LANES, cz * j % LANES
            total = jnp.zeros((ngx, LANES), F32)
            for f in range(2):
                piece = tx[f][:, c * LANES : (c + 1) * LANES]
                if low + cz > LANES:
                    after = tx[f][:, (c + 1) * LANES : (c + 2) * LANES]
                    piece = jnp.where(lane >= low, piece, after)
                piece = pltpu.roll(piece, (cz * f - low) % LANES, 1)
                total = jnp.where((lane >= cz * f) & (lane < cz * (f + 1)), piece, total)
            out[pl.ds(j * per + m, ngx, stride=ngz * per), :] = total
        for i in range(ngx):
            c, low = cx * i // LANES, cx * i % LANES
            rows = pl.ds(i * ngz * per + m, ngz, stride=per)
            total = out[rows, :]
            for f in range(2):
                start = 2 * cz + cx * f
                piece = pltpu.roll(tz[f][:, c * LANES : (c + 1) * LANES], (start - low) % LANES, 1)
                total = jnp.where((lane8 >= start) & (lane8 < start + cx), piece, total)
            out[rows, :] = total


def backward_kernel(
    u, v, w, ul, uh, wl, wh, got, modes, sa, ca, sb, cb, sx, sz, eth, etl, mux, mum,
    pressure, u_new, v_new, w_new, sh, sl, kh, kl, fh, fl, ring, plow, phigh,
):
    cx, cz, ny = u.shape
    cells = cx * cz
    fill_sine((sa, ca, sb, cb), sh, sl)
    fill_local(sx, sz, kh, kl)

    @pl.loop(0, ny // TILE)
    def _(n):
        cols = pl.ds(pl.multiple_of(n * TILE, TILE), TILE)
        edge = split(got[cols, :].T)
        field = dot3((eth[...], etl[...]), edge) - modes[:, cols]
        field = split(field / (mux[...] + mum[:, cols]))
        field = split(dot3((kh[...], kl[...]), field))
        fh[:cells, cols], fl[:cells, cols] = field
        fh[cells:, cols], fl[cells:, cols] = edge

    @pl.loop(0, ny // TILE)
    def _(n):
        cols = pl.ds(pl.multiple_of(n * TILE, TILE), TILE)
        wide = dot3((fh[...], fl[...]), (sh[:, cols], sl[:, cols]))
        pressure[:, :, cols] = wide[:cells].reshape(cx, cz, TILE)
        ring[:, cols] = wide[cells:]

    plow[...] = ring[:cz, :] - 0.5 * ul[...].astype(F32)
    phigh[...] = ring[cz : 2 * cz, :] + 0.5 * uh[...].astype(F32)
    edge = pl.ds(2 * cz, cx)
    ring[edge, :] = ring[edge, :] - 0.5 * wl[...].astype(F32)
    edge = pl.ds(2 * cz + cx, cx)
    ring[edge, :] = ring[edge, :] + 0.5 * wh[...].astype(F32)

    def finish(x, before, after):
        here = pressure[x]
        u_new[x] = u[x].astype(F32) - 0.5 * (after - before)
        v_new[x] = v[x].astype(F32) - 0.5 * along_lanes(here)
        first = ring[pl.ds(2 * cz + x, 1), :]
        last = ring[pl.ds(2 * cz + cx + x, 1), :]
        w_new[x] = w[x].astype(F32) - 0.5 * along_rows(here, first, last)

    finish(0, plow[...], pressure[1])
    finish(cx - 1, pressure[cx - 2], phigh[...])

    @pl.loop(1, cx - 1)
    def _(x):
        finish(x, pressure[x - 1], pressure[x + 1])


def call(kernel, name, outs, scratch, flops, *args, places=(), effects=False):
    spaces = dict(places)
    size = sum(math.prod(a.shape) * a.dtype.itemsize for a in [*args, *outs])
    return pl.pallas_call(
        kernel,
        out_shape=outs,
        in_specs=[
            pl.BlockSpec(memory_space=spaces.get(i, pltpu.VMEM)) for i in range(len(args))
        ],
        out_specs=[pl.BlockSpec(memory_space=pltpu.VMEM)] * len(outs),
        scratch_shapes=scratch,
        compiler_params=pltpu.CompilerParams(
            vmem_limit_bytes=60 << 20, has_side_effects=effects
        ),
        cost_estimate=pl.CostEstimate(flops=flops, bytes_accessed=size, transcendentals=0),
        name=name,
    )(*args)


def on_device(u_vel, v_vel, w_vel):
    cx, cz, ny = u_vel.shape
    ngx = lax.axis_size("gx")
    ngz = lax.axis_size("gz")
    nx, nz = ngx * cx, ngz * cz
    devices = ngx * ngz
    per = ny // devices
    cells = cx * cz
    edges = 2 * (cx + cz)
    local = np.kron(sine_np(cx), sine_np(cz))[edge_rows(cx, cz)]
    tables = [f32(t) for t in sine_parts_np(ny, 32)]
    tables += [f32(np.repeat(sine_np(cx), cz, 1)), f32(np.tile(sine_np(cz), (1, cx)))]
    mux = f32(np.add.outer(wall_eigen_np(cx), wall_eigen_np(cz)).reshape(-1, 1))
    mum = f32(wall_eigen_np(ny).reshape(1, -1))
    shape = jax.ShapeDtypeStruct
    square = [pltpu.VMEM((ny, ny), BF16)] * 2 + [pltpu.VMEM((cells, cells), BF16)] * 2
    u_edge, w_edge = shape((cz, ny), BF16), shape((cx, ny), BF16)
    send, modes, w_first, w_last = call(
        forward_kernel,
        "forward",
        [shape((ny, edges), F32), shape((cells, ny), F32), w_edge, w_edge],
        square + [pltpu.VMEM((cells + edges, ny), BF16), pltpu.VMEM((cells, ny), BF16)],
        6 * cells * ny * (ny + cells + edges),
        u_vel, v_vel, w_vel, *tables, *halves(local), mux, mum,
    )
    rows = shape((ny, 1, edges), F32)
    sems = [pltpu.SemaphoreType.DMA] * 3
    seen, u_low, u_high, w_low, w_high = call(
        exchange_halo_kernel,
        "exchange_halo",
        [rows, u_edge, u_edge, w_edge, w_edge],
        sems + [pltpu.SemaphoreType.DMA((4,))] * 2,
        0,
        send.reshape(ny, 1, edges), u_vel, w_first, w_last,
        places={1: pl.ANY},
        effects=True,
    )
    hx, hz = hartley_np(nx), hartley_np(nz)
    block_x, block_z = np.arange(ngx) * cx, np.arange(ngz) * cz
    lx = hx[:, np.concatenate([(block_x - 1) % nx, (block_x + cx) % nx])]
    lz = hz[:, np.concatenate([(block_z - 1) % nz, (block_z + cz) % nz])]
    (back,) = call(
        functools.partial(owner_kernel, ngx, ngz, cx, cz),
        "owner",
        [shape((ny, edges), F32)],
        [],
        6 * per * nx * nz * 200,
        seen.reshape(ny, edges),
        *halves(hx), *halves(hz), *halves(lx), *halves(lx.T), *halves(lz.T),
        f32(periodic_eigen_np(nz).reshape(1, -1)),
        f32(periodic_eigen_np(nx).reshape(-1, 1)),
        f32(mum[0]),
        places={13: pltpu.SMEM},
    )
    (got,) = call(
        exchange_kernel, "exchange", [rows], sems, 0, back.reshape(ny, 1, edges), effects=True
    )
    block = shape((cx, cz, ny), F32)
    return tuple(
        call(
            backward_kernel,
            "backward",
            [block] * 4,
            square
            + [pltpu.VMEM((cells + edges, ny), BF16)] * 2
            + [pltpu.VMEM((edges, ny), F32)]
            + [pltpu.VMEM((cz, ny), F32)] * 2,
            6 * cells * ny * (ny + cells + edges),
            u_vel, v_vel, w_vel, u_low, u_high, w_low, w_high, got.reshape(ny, edges), modes,
            *tables, *halves(local.T), mux, mum,
        )
    )


def solution(mesh):
    spec = P("gx", "gz", None)
    return jax.shard_map(
        on_device, mesh=mesh, in_specs=(spec,) * 3, out_specs=(spec,) * 4, check_vma=False
    )
```

```python
import functools
import math

import jax
import jax.numpy as jnp
import numpy as np
from jax import lax
from jax.experimental import pallas as pl
from jax.experimental.pallas import tpu as pltpu
from jax.sharding import PartitionSpec as P

F32 = jnp.float32
BF16 = jnp.bfloat16
TILE = 256
LANES = 128


def hartley_np(count):
    index = np.arange(count)
    angle = (index[:, None] * index[None, :] % count) * (2.0 * np.pi / count)
    return np.cos(angle) + np.sin(angle)


def sine_np(count):
    index = np.arange(1, count + 1)
    angle = (index[:, None] * index[None, :] % (2 * (count + 1))) * (np.pi / (count + 1))
    return np.sqrt(2.0 / (count + 1)) * np.sin(angle)


def sine_parts_np(count, step):
    mode = np.arange(1, count + 1)
    coarse = np.arange(0, count, step)
    fine = np.arange(1, step + 1)
    size = np.sqrt(2.0 / (count + 1))
    angle_c = (coarse[:, None] * mode % (2 * (count + 1))) * (np.pi / (count + 1))
    angle_f = (fine[:, None] * mode % (2 * (count + 1))) * (np.pi / (count + 1))
    return (
        size * np.sin(angle_c),
        size * np.cos(angle_c),
        np.sin(angle_f),
        np.cos(angle_f),
    )


def wall_eigen_np(count):
    return 4.0 * np.sin(np.arange(1, count + 1) * (np.pi / (2 * count + 2))) ** 2


def periodic_eigen_np(count):
    return 4.0 * np.sin(np.arange(count) * (np.pi / count)) ** 2


def edge_rows(cx, cz):
    grid = np.arange(cx * cz).reshape(cx, cz)
    return np.concatenate([grid[0], grid[-1], grid[:, 0], grid[:, -1]])


def f32(array):
    return np.ascontiguousarray(np.asarray(array, np.float32))


def halves(array):
    array = np.asarray(array, np.float32)
    high = array.astype(BF16)
    low = (array - high.astype(np.float32)).astype(BF16)
    return [high, low]


def split(x):
    high = x.astype(BF16)
    return high, (x - high.astype(F32)).astype(BF16)


def dot(a, b):
    return jnp.dot(a, b, preferred_element_type=F32)


def dot_t(a, b):
    return lax.dot_general(a, b, (((1,), (1,)), ((), ())), preferred_element_type=F32)


def dot3(a, b, op=dot):
    return op(a[0], b[0]) + op(a[1], b[0]) + op(a[0], b[1])


def fill_sine(parts, high, low):
    sa, ca, sb, cb = parts
    step = sb.shape[0]

    @pl.loop(0, sa.shape[0])
    def _(a):
        block = sa[pl.ds(a, 1), :] * cb[...] + ca[pl.ds(a, 1), :] * sb[...]
        rows = pl.ds(pl.multiple_of(a * step, step), step)
        high[rows, :], low[rows, :] = split(block)


def fill_local(sx, sz, high, low):
    step = sz.shape[0]

    @pl.loop(0, sx.shape[0])
    def _(a):
        rows = pl.ds(pl.multiple_of(a * step, step), step)
        high[rows, :], low[rows, :] = split(sx[pl.ds(a, 1), :] * sz[...])


def along_rows(x, first, last):
    rows = x.shape[0]
    at = lax.broadcasted_iota(jnp.int32, x.shape, 0)
    up = jnp.where(at == rows - 1, last, pltpu.roll(x, rows - 1, 0))
    down = jnp.where(at == 0, first, pltpu.roll(x, 1, 0))
    return up - down


def along_lanes(x):
    lanes = x.shape[1]
    at = lax.broadcasted_iota(jnp.int32, x.shape, 1)
    up = jnp.where(at == lanes - 1, 0.0, pltpu.roll(x, lanes - 1, 1))
    down = jnp.where(at == 0, 0.0, pltpu.roll(x, 1, 1))
    return up - down


def arrivals(pairs, sems):
    copies = [pltpu.make_async_copy(a, b, sems.at[i]) for i, (a, b) in enumerate(pairs)]
    for c in copies:
        c.start()
    return copies


def tile_copy(source, target, sems, n):
    cols = pl.ds(pl.multiple_of(n * TILE, TILE), TILE)
    return pltpu.make_async_copy(source.at[..., cols], target.at[..., cols], sems.at[n])


def forward_kernel(
    u_hbm, v_hbm, w_hbm, sa, ca, sb, cb, sx, sz, eh, el, mux, mum, send, modes_hbm,
    sh, sl, kh, kl, dh, dl, u, v, w, modes, in_sem, out_sem,
):
    cx, cz, ny = u.shape
    cells = cx * cz
    arrive = arrivals([(u_hbm, u), (v_hbm, v), (w_hbm, w)], in_sem)
    fill_sine((sa, ca, sb, cb), sh, sl)
    fill_local(sx, sz, kh, kl)
    for c in arrive:
        c.wait()

    @pl.loop(0, cx)
    def _(x):
        after = u[jnp.minimum(x + 1, cx - 1)].astype(F32) * jnp.where(x < cx - 1, 1.0, 0.0)
        before = u[jnp.maximum(x - 1, 0)].astype(F32) * jnp.where(x > 0, 1.0, 0.0)
        div = 0.5 * (
            (after - before)
            + along_lanes(v[x].astype(F32))
            + along_rows(w[x].astype(F32), 0.0, 0.0)
        )
        rows = pl.ds(pl.multiple_of(x * cz, cz), cz)
        dh[rows, :], dl[rows, :] = split(div)

    dh[cells : cells + cz, :] = (-0.5 * u[0].astype(F32)).astype(BF16)
    dh[cells + cz : cells + 2 * cz, :] = (0.5 * u[cx - 1].astype(F32)).astype(BF16)
    dh[cells + 2 * cz : cells + 2 * cz + cx, :] = (-0.5 * w[:, 0, :].astype(F32)).astype(BF16)
    dh[cells + 2 * cz + cx :, :] = (0.5 * w[:, cz - 1, :].astype(F32)).astype(BF16)

    @pl.loop(0, ny // TILE)
    def _(n):
        cols = pl.ds(pl.multiple_of(n * TILE, TILE), TILE)
        wide = dot(dh[...], sh[:, cols]) + dot(dh[...], sl[:, cols])
        field = wide[:cells] + dot(dl[...], sh[:, cols])
        mode = dot3((kh[...], kl[...]), split(field))
        modes[:, cols] = mode
        mode = mode / (mux[...] + mum[:, cols])
        edge = wide[cells:] - dot3((eh[...], el[...]), split(mode))
        send[cols, :] = edge.T
        tile_copy(modes, modes_hbm, out_sem, n).start()

    @pl.loop(0, ny // TILE)
    def _(n):
        tile_copy(modes, modes_hbm, out_sem, n).wait()


def owner_kernel(
    ngx, ngz, cx, cz, seen, hxh, hxl, hzh, hzl, lxh, lxl, lxth, lxtl, lzth, lztl, muz, mukx, mum, out
):
    per = mum.shape[0]
    nx, nz = ngx * cx, ngz * cz
    lane = lax.broadcasted_iota(jnp.int32, (ngx, LANES), 1)
    lane8 = lax.broadcasted_iota(jnp.int32, (ngz, LANES), 1)
    wide_x = nz // LANES
    wide_z = nx // LANES
    hx = (hxh[...], hxl[...])
    hz = (hzh[...], hzl[...])
    px, pz = [], []
    for m in range(per):
        cols = [[jnp.zeros((ngx, LANES), F32)] * wide_x for _ in range(2)]
        for j in range(ngz):
            piece = seen[pl.ds(j * per + m, ngx, stride=ngz * per), :]
            for f in range(2):
                turned = pltpu.roll(piece, (cz * j - cz * f) % LANES, 1)
                for c in range(wide_x):
                    low, high = cz * j - c * LANES, cz * (j + 1) - c * LANES
                    if high > 0 and low < LANES:
                        cols[f][c] = jnp.where((lane >= low) & (lane < high), turned, cols[f][c])
        px += [jnp.concatenate(c, 1) for c in cols]
        cols = [[jnp.zeros((ngz, LANES), F32)] * wide_z for _ in range(2)]
        for i in range(ngx):
            piece = seen[pl.ds(i * ngz * per + m, ngz, stride=per), :]
            c, low = cx * i // LANES, cx * i % LANES
            for f in range(2):
                turned = pltpu.roll(piece, (low - 2 * cz - cx * f) % LANES, 1)
                cols[f][c] = jnp.where((lane8 >= low) & (lane8 < low + cx), turned, cols[f][c])
        pz += [jnp.concatenate(c, 1) for c in cols]
    f1 = dot3(split(jnp.concatenate(px, 0)), hz)
    f2 = dot3(split(jnp.concatenate(pz, 0)), hx)
    ex, ez = [], []
    for m in range(per):
        mine = f1[2 * ngx * m : 2 * ngx * (m + 1)]
        other = f2[2 * ngz * m : 2 * ngz * (m + 1)].T
        spec = dot3((lxh[...], lxl[...]), split(mine)) + dot3(split(other), (lzth[...], lztl[...]))
        spec = spec / ((mukx[...] + muz[...] + mum[m : m + 1, :1]) * (-float(nx * nz)))
        spec = split(spec)
        ex.append(dot3((lxth[...], lxtl[...]), spec))
        ez.append(dot3((lzth[...], lztl[...]), spec, dot_t))
    ex = -dot3(split(jnp.concatenate(ex, 0)), hz)
    ez = -dot3(split(jnp.concatenate(ez, 0)), hx)
    for m in range(per):
        tx, tz = [], []
        for f in range(2):
            at = 2 * ngx * m + f * ngx
            turn = 1 if f == 0 else ngx - 1
            tx.append(ex[at : at + ngx] + pltpu.roll(px[2 * m + 1 - f], turn, 0))
            at = 2 * ngz * m + f * ngz
            turn = 1 if f == 0 else ngz - 1
            tz.append(ez[at : at + ngz] + pltpu.roll(pz[2 * m + 1 - f], turn, 0))
        for j in range(ngz):
            c, low = cz * j // LANES, cz * j % LANES
            total = jnp.zeros((ngx, LANES), F32)
            for f in range(2):
                piece = tx[f][:, c * LANES : (c + 1) * LANES]
                if low + cz > LANES:
                    after = tx[f][:, (c + 1) * LANES : (c + 2) * LANES]
                    piece = jnp.where(lane >= low, piece, after)
                piece = pltpu.roll(piece, (cz * f - low) % LANES, 1)
                total = jnp.where((lane >= cz * f) & (lane < cz * (f + 1)), piece, total)
            out[pl.ds(j * per + m, ngx, stride=ngz * per), :] = total
        for i in range(ngx):
            c, low = cx * i // LANES, cx * i % LANES
            rows = pl.ds(i * ngz * per + m, ngz, stride=per)
            total = out[rows, :]
            for f in range(2):
                start = 2 * cz + cx * f
                piece = pltpu.roll(tz[f][:, c * LANES : (c + 1) * LANES], (start - low) % LANES, 1)
                total = jnp.where((lane8 >= start) & (lane8 < start + cx), piece, total)
            out[rows, :] = total


def backward_kernel(
    u_hbm, v_hbm, w_hbm, ul, uh, wl, wh, got, modes_hbm, sa, ca, sb, cb, sx, sz, eth, etl, mux, mum,
    pressure_hbm, u_out, v_out, w_out, sh, sl, kh, kl, fh, fl, ring, plow, phigh,
    u, v, w, modes, pressure, u_new, v_new, w_new, in_sem, p_sem, out_sem,
):
    cx, cz, ny = u.shape
    cells = cx * cz
    arrive = arrivals([(modes_hbm, modes), (u_hbm, u), (v_hbm, v), (w_hbm, w)], in_sem)
    fill_sine((sa, ca, sb, cb), sh, sl)
    fill_local(sx, sz, kh, kl)

    arrive[0].wait()

    @pl.loop(0, ny // TILE)
    def _(n):
        cols = pl.ds(pl.multiple_of(n * TILE, TILE), TILE)
        edge = split(got[cols, :].T)
        field = dot3((eth[...], etl[...]), edge) - modes[:, cols]
        field = split(field / (mux[...] + mum[:, cols]))
        field = split(dot3((kh[...], kl[...]), field))
        fh[:cells, cols], fl[:cells, cols] = field
        fh[cells:, cols], fl[cells:, cols] = edge

    @pl.loop(0, ny // TILE)
    def _(n):
        cols = pl.ds(pl.multiple_of(n * TILE, TILE), TILE)
        wide = dot3((fh[...], fl[...]), (sh[:, cols], sl[:, cols]))
        pressure[:, :, cols] = wide[:cells].reshape(cx, cz, TILE)
        ring[:, cols] = wide[cells:]

        @pl.when(n > 0)
        def _():
            tile_copy(pressure, pressure_hbm, p_sem, n - 1).start()

    for c in arrive[1:]:
        c.wait()

    plow[...] = ring[:cz, :] - 0.5 * ul[...].astype(F32)
    phigh[...] = ring[cz : 2 * cz, :] + 0.5 * uh[...].astype(F32)
    edge = pl.ds(2 * cz, cx)
    ring[edge, :] = ring[edge, :] - 0.5 * wl[...].astype(F32)
    edge = pl.ds(2 * cz + cx, cx)
    ring[edge, :] = ring[edge, :] + 0.5 * wh[...].astype(F32)

    def finish(x, before, after):
        here = pressure[x]
        u_new[x] = u[x].astype(F32) - 0.5 * (after - before)
        v_new[x] = v[x].astype(F32) - 0.5 * along_lanes(here)
        first = ring[pl.ds(2 * cz + x, 1), :]
        last = ring[pl.ds(2 * cz + cx + x, 1), :]
        w_new[x] = w[x].astype(F32) - 0.5 * along_rows(here, first, last)

    def leave(x):
        planes = [(u_new, u_out), (v_new, v_out), (w_new, w_out)]
        return [
            pltpu.make_async_copy(a.at[x], b.at[x], out_sem.at[i, x])
            for i, (a, b) in enumerate(planes)
        ]

    finish(0, plow[...], pressure[1])
    finish(cx - 1, pressure[cx - 2], phigh[...])
    tile_copy(pressure, pressure_hbm, p_sem, ny // TILE - 1).start()

    @pl.loop(1, cx - 1)
    def _(x):
        finish(x, pressure[x - 1], pressure[x + 1])
        for c in leave(x - 1):
            c.start()

    for x in (cx - 1, cx - 2):
        for c in leave(x):
            c.start()

    @pl.loop(0, ny // TILE)
    def _(n):
        tile_copy(pressure, pressure_hbm, p_sem, n).wait()

    @pl.loop(0, cx)
    def _(x):
        for c in leave(x):
            c.wait()


def _(x):
        finish(x, pressure[x - 1], pressure[x + 1])


def shifted(block, axis, step):
    count = lax.axis_size(axis)
    return lax.ppermute(block, axis, [(i, (i + step) % count) for i in range(count)])


def call(kernel, name, outs, scratch, flops, *args, places=(), out_places=()):
    spaces, out_spaces = dict(places), dict(out_places)
    size = sum(math.prod(a.shape) * a.dtype.itemsize for a in [*args, *outs])
    return pl.pallas_call(
        kernel,
        out_shape=outs,
        in_specs=[
            pl.BlockSpec(memory_space=spaces.get(i, pltpu.VMEM)) for i in range(len(args))
        ],
        out_specs=[
            pl.BlockSpec(memory_space=out_spaces.get(i, pltpu.VMEM)) for i in range(len(outs))
        ],
        scratch_shapes=scratch,
        compiler_params=pltpu.CompilerParams(vmem_limit_bytes=60 << 20),
        cost_estimate=pl.CostEstimate(flops=flops, bytes_accessed=size, transcendentals=0),
        name=name,
    )(*args)


def on_device(u_vel, v_vel, w_vel):
    cx, cz, ny = u_vel.shape
    ngx = lax.axis_size("gx")
    ngz = lax.axis_size("gz")
    nx, nz = ngx * cx, ngz * cz
    devices = ngx * ngz
    per = ny // devices
    cells = cx * cz
    edges = 2 * (cx + cz)
    me = lax.axis_index("gx") * ngz + lax.axis_index("gz")
    u_low = shifted(u_vel[-1], "gx", 1)
    u_high = shifted(u_vel[0], "gx", -1)
    w_low = shifted(w_vel[:, -1], "gz", 1)
    w_high = shifted(w_vel[:, 0], "gz", -1)
    local = np.kron(sine_np(cx), sine_np(cz))[edge_rows(cx, cz)]
    tables = [f32(t) for t in sine_parts_np(ny, 32)]
    tables += [f32(np.repeat(sine_np(cx), cz, 1)), f32(np.tile(sine_np(cz), (1, cx)))]
    mux = f32(np.add.outer(wall_eigen_np(cx), wall_eigen_np(cz)).reshape(-1, 1))
    mum = f32(wall_eigen_np(ny).reshape(1, -1))
    shape = jax.ShapeDtypeStruct
    square = [pltpu.VMEM((ny, ny), BF16)] * 2 + [pltpu.VMEM((cells, cells), BF16)] * 2
    planes = [pltpu.VMEM((cx, cz, ny), BF16)] * 3
    send, modes = call(
        forward_kernel,
        "forward",
        [shape((ny, edges), F32), shape((cells, ny), F32)],
        square
        + [pltpu.VMEM((cells + edges, ny), BF16), pltpu.VMEM((cells, ny), BF16)]
        + planes
        + [pltpu.VMEM((cells, ny), F32)]
        + [pltpu.SemaphoreType.DMA((3,)), pltpu.SemaphoreType.DMA((ny // TILE,))],
        6 * cells * ny * (ny + cells + edges),
        u_vel, v_vel, w_vel, *tables, *halves(local), mux, mum,
        places={i: pl.ANY for i in range(3)},
        out_places={1: pl.ANY},
    )
    send = send.reshape(devices, per, 1, edges)
    seen = lax.all_to_all(send, ("gx", "gz"), split_axis=0, concat_axis=0, tiled=True)
    hx, hz = hartley_np(nx), hartley_np(nz)
    block_x, block_z = np.arange(ngx) * cx, np.arange(ngz) * cz
    lx = hx[:, np.concatenate([(block_x - 1) % nx, (block_x + cx) % nx])]
    lz = hz[:, np.concatenate([(block_z - 1) % nz, (block_z + cz) % nz])]
    lam_m = lax.dynamic_slice(jnp.asarray(mum[0]), (me * per,), (per,))
    (back,) = call(
        functools.partial(owner_kernel, ngx, ngz, cx, cz),
        "owner",
        [shape((ny, edges), F32)],
        [],
        6 * per * nx * nz * 200,
        seen.reshape(ny, edges),
        *halves(hx), *halves(hz), *halves(lx), *halves(lx.T), *halves(lz.T),
        f32(periodic_eigen_np(nz).reshape(1, -1)),
        f32(periodic_eigen_np(nx).reshape(-1, 1)),
        jnp.broadcast_to(lam_m[:, None], (per, LANES)),
    )
    back = back.reshape(devices, per, 1, edges)
    got = lax.all_to_all(back, ("gx", "gz"), split_axis=0, concat_axis=0, tiled=True)
    block = shape((cx, cz, ny), F32)
    return tuple(
        call(
            backward_kernel,
            "backward",
            [block] * 4,
            square
            + [pltpu.VMEM((cells + edges, ny), BF16)] * 2
            + [pltpu.VMEM((edges, ny), F32)]
            + [pltpu.VMEM((cz, ny), F32)] * 2
            + planes
            + [pltpu.VMEM((cells, ny), F32)]
            + [pltpu.VMEM((cx, cz, ny), F32)] * 4
            + [pltpu.SemaphoreType.DMA((4,)), pltpu.SemaphoreType.DMA((ny // TILE,))]
            + [pltpu.SemaphoreType.DMA((3, cx))],
            6 * cells * ny * (ny + cells + edges),
            u_vel, v_vel, w_vel, u_low, u_high, w_low, w_high, got.reshape(ny, edges), modes,
            *tables, *halves(local.T), mux, mum,
            places={i: pl.ANY for i in (0, 1, 2, 8)},
            out_places={i: pl.ANY for i in range(4)},
        )
    )


def solution(mesh):
    spec = P("gx", "gz", None)
    return jax.shard_map(
        on_device, mesh=mesh, in_specs=(spec,) * 3, out_specs=(spec,) * 4, check_vma=False
    )
```

```python
import functools
import math

import jax
import jax.numpy as jnp
import numpy as np
from jax import lax
from jax.experimental import pallas as pl
from jax.experimental.pallas import tpu as pltpu
from jax.sharding import PartitionSpec as P

F32 = jnp.float32
BF16 = jnp.bfloat16
TILE = 256
LANES = 128


def hartley_np(count):
    index = np.arange(count)
    angle = (index[:, None] * index[None, :] % count) * (2.0 * np.pi / count)
    return np.cos(angle) + np.sin(angle)


def sine_np(count):
    index = np.arange(1, count + 1)
    angle = (index[:, None] * index[None, :] % (2 * (count + 1))) * (np.pi / (count + 1))
    return np.sqrt(2.0 / (count + 1)) * np.sin(angle)


def sine_parts_np(count, step):
    mode = np.arange(1, count + 1)
    coarse = np.arange(0, count, step)
    fine = np.arange(1, step + 1)
    size = np.sqrt(2.0 / (count + 1))
    angle_c = (coarse[:, None] * mode % (2 * (count + 1))) * (np.pi / (count + 1))
    angle_f = (fine[:, None] * mode % (2 * (count + 1))) * (np.pi / (count + 1))
    return (
        size * np.sin(angle_c),
        size * np.cos(angle_c),
        np.sin(angle_f),
        np.cos(angle_f),
    )


def wall_eigen_np(count):
    return 4.0 * np.sin(np.arange(1, count + 1) * (np.pi / (2 * count + 2))) ** 2


def periodic_eigen_np(count):
    return 4.0 * np.sin(np.arange(count) * (np.pi / count)) ** 2


def edge_rows(cx, cz):
    grid = np.arange(cx * cz).reshape(cx, cz)
    return np.concatenate([grid[0], grid[-1], grid[:, 0], grid[:, -1]])


def f32(array):
    return np.ascontiguousarray(np.asarray(array, np.float32))


def halves(array):
    array = np.asarray(array, np.float32)
    high = array.astype(BF16)
    low = (array - high.astype(np.float32)).astype(BF16)
    return [high, low]


def split(x):
    high = x.astype(BF16)
    return high, (x - high.astype(F32)).astype(BF16)


def dot(a, b):
    return jnp.dot(a, b, preferred_element_type=F32)


def dot_t(a, b):
    return lax.dot_general(a, b, (((1,), (1,)), ((), ())), preferred_element_type=F32)


def dot3(a, b, op=dot):
    return op(a[0], b[0]) + op(a[1], b[0]) + op(a[0], b[1])


def fill_sine(parts, high, low):
    sa, ca, sb, cb = parts
    step = sb.shape[0]

    @pl.loop(0, sa.shape[0])
    def _(a):
        block = sa[pl.ds(a, 1), :] * cb[...] + ca[pl.ds(a, 1), :] * sb[...]
        rows = pl.ds(pl.multiple_of(a * step, step), step)
        high[rows, :], low[rows, :] = split(block)


def fill_local(sx, sz, high, low):
    step = sz.shape[0]

    @pl.loop(0, sx.shape[0])
    def _(a):
        rows = pl.ds(pl.multiple_of(a * step, step), step)
        high[rows, :], low[rows, :] = split(sx[pl.ds(a, 1), :] * sz[...])


def by_parity(high, low, field):
    half = field.shape[0] // 2
    parts = []
    for part in (slice(0, half), slice(half, 2 * half)):
        parts.append(dot3((high[part, :], low[part, :]), split(field[part])))
    return jnp.concatenate(parts, 0)


def along_rows(x, first, last):
    rows = x.shape[0]
    at = lax.broadcasted_iota(jnp.int32, x.shape, 0)
    up = jnp.where(at == rows - 1, last, pltpu.roll(x, rows - 1, 0))
    down = jnp.where(at == 0, first, pltpu.roll(x, 1, 0))
    return up - down


def along_lanes(x):
    lanes = x.shape[1]
    at = lax.broadcasted_iota(jnp.int32, x.shape, 1)
    up = jnp.where(at == lanes - 1, 0.0, pltpu.roll(x, lanes - 1, 1))
    down = jnp.where(at == 0, 0.0, pltpu.roll(x, 1, 1))
    return up - down


def arrivals(pairs, sems):
    copies = [pltpu.make_async_copy(a, b, sems.at[i]) for i, (a, b) in enumerate(pairs)]
    for c in copies:
        c.start()
    return copies


def tile_copy(source, target, sems, n):
    cols = pl.ds(pl.multiple_of(n * TILE, TILE), TILE)
    return pltpu.make_async_copy(source.at[..., cols], target.at[..., cols], sems.at[n])


def forward_kernel(
    u_hbm, v_hbm, w_hbm, sa, ca, sb, cb, sx, sz, eh, el, mux, mum, send, modes_hbm,
    sh, sl, kh, kl, dh, dl, u, v, w, modes, in_sem, out_sem,
):
    cx, cz, ny = u.shape
    cells = cx * cz
    arrive = arrivals([(u_hbm, u), (v_hbm, v), (w_hbm, w)], in_sem)
    fill_sine((sa, ca, sb, cb), sh, sl)
    fill_local(sx, sz, kh, kl)
    for c in arrive:
        c.wait()

    def divergence(x):
        after = u[jnp.minimum(x + 1, cx - 1)].astype(F32) * jnp.where(x < cx - 1, 1.0, 0.0)
        before = u[jnp.maximum(x - 1, 0)].astype(F32) * jnp.where(x > 0, 1.0, 0.0)
        return 0.5 * (
            (after - before)
            + along_lanes(v[x].astype(F32))
            + along_rows(w[x].astype(F32), 0.0, 0.0)
        )

    @pl.loop(0, cx // 2)
    def _(x):
        left, right = divergence(x), divergence(cx - 1 - x)
        rows = pl.ds(pl.multiple_of(x * cz, cz), cz)
        dh[rows, :], dl[rows, :] = split(left + right)
        rows = pl.ds(pl.multiple_of(cells // 2 + x * cz, cz), cz)
        dh[rows, :], dl[rows, :] = split(left - right)

    dh[cells : cells + cz, :] = (-0.5 * u[0].astype(F32)).astype(BF16)
    dh[cells + cz : cells + 2 * cz, :] = (0.5 * u[cx - 1].astype(F32)).astype(BF16)
    dh[cells + 2 * cz : cells + 2 * cz + cx, :] = (-0.5 * w[:, 0, :].astype(F32)).astype(BF16)
    dh[cells + 2 * cz + cx :, :] = (0.5 * w[:, cz - 1, :].astype(F32)).astype(BF16)

    @pl.loop(0, ny // TILE)
    def _(n):
        cols = pl.ds(pl.multiple_of(n * TILE, TILE), TILE)
        wide = dot(dh[...], sh[:, cols]) + dot(dh[...], sl[:, cols])
        field = wide[:cells] + dot(dl[...], sh[:, cols])
        mode = by_parity(kh, kl, field)
        modes[:, cols] = mode
        mode = mode / (mux[...] + mum[:, cols])
        edge = wide[cells:] - dot3((eh[...], el[...]), split(mode))
        send[cols, :] = edge.T
        tile_copy(modes, modes_hbm, out_sem, n).start()

    @pl.loop(0, ny // TILE)
    def _(n):
        tile_copy(modes, modes_hbm, out_sem, n).wait()


def owner_kernel(
    ngx, ngz, cx, cz, seen, hxh, hxl, hzh, hzl, lxh, lxl, lxth, lxtl, lzth, lztl, muz, mukx, mum, out
):
    per = mum.shape[0]
    nx, nz = ngx * cx, ngz * cz
    lane = lax.broadcasted_iota(jnp.int32, (ngx, LANES), 1)
    lane8 = lax.broadcasted_iota(jnp.int32, (ngz, LANES), 1)
    wide_x = nz // LANES
    wide_z = nx // LANES
    hx = (hxh[...], hxl[...])
    hz = (hzh[...], hzl[...])
    px, pz = [], []
    for m in range(per):
        cols = [[jnp.zeros((ngx, LANES), F32)] * wide_x for _ in range(2)]
        for j in range(ngz):
            piece = seen[pl.ds(j * per + m, ngx, stride=ngz * per), :]
            for f in range(2):
                turned = pltpu.roll(piece, (cz * j - cz * f) % LANES, 1)
                for c in range(wide_x):
                    low, high = cz * j - c * LANES, cz * (j + 1) - c * LANES
                    if high > 0 and low < LANES:
                        cols[f][c] = jnp.where((lane >= low) & (lane < high), turned, cols[f][c])
        px += [jnp.concatenate(c, 1) for c in cols]
        cols = [[jnp.zeros((ngz, LANES), F32)] * wide_z for _ in range(2)]
        for i in range(ngx):
            piece = seen[pl.ds(i * ngz * per + m, ngz, stride=per), :]
            c, low = cx * i // LANES, cx * i % LANES
            for f in range(2):
                turned = pltpu.roll(piece, (low - 2 * cz - cx * f) % LANES, 1)
                cols[f][c] = jnp.where((lane8 >= low) & (lane8 < low + cx), turned, cols[f][c])
        pz += [jnp.concatenate(c, 1) for c in cols]
    f1 = dot3(split(jnp.concatenate(px, 0)), hz)
    f2 = dot3(split(jnp.concatenate(pz, 0)), hx)
    ex, ez = [], []
    for m in range(per):
        mine = f1[2 * ngx * m : 2 * ngx * (m + 1)]
        other = f2[2 * ngz * m : 2 * ngz * (m + 1)].T
        spec = dot3((lxh[...], lxl[...]), split(mine)) + dot3(split(other), (lzth[...], lztl[...]))
        spec = spec / ((mukx[...] + muz[...] + mum[m : m + 1, :1]) * (-float(nx * nz)))
        spec = split(spec)
        ex.append(dot3((lxth[...], lxtl[...]), spec))
        ez.append(dot3((lzth[...], lztl[...]), spec, dot_t))
    ex = -dot3(split(jnp.concatenate(ex, 0)), hz)
    ez = -dot3(split(jnp.concatenate(ez, 0)), hx)
    for m in range(per):
        tx, tz = [], []
        for f in range(2):
            at = 2 * ngx * m + f * ngx
            turn = 1 if f == 0 else ngx - 1
            tx.append(ex[at : at + ngx] + pltpu.roll(px[2 * m + 1 - f], turn, 0))
            at = 2 * ngz * m + f * ngz
            turn = 1 if f == 0 else ngz - 1
            tz.append(ez[at : at + ngz] + pltpu.roll(pz[2 * m + 1 - f], turn, 0))
        for j in range(ngz):
            c, low = cz * j // LANES, cz * j % LANES
            total = jnp.zeros((ngx, LANES), F32)
            for f in range(2):
                piece = tx[f][:, c * LANES : (c + 1) * LANES]
                if low + cz > LANES:
                    after = tx[f][:, (c + 1) * LANES : (c + 2) * LANES]
                    piece = jnp.where(lane >= low, piece, after)
                piece = pltpu.roll(piece, (cz * f - low) % LANES, 1)
                total = jnp.where((lane >= cz * f) & (lane < cz * (f + 1)), piece, total)
            out[pl.ds(j * per + m, ngx, stride=ngz * per), :] = total
        for i in range(ngx):
            c, low = cx * i // LANES, cx * i % LANES
            rows = pl.ds(i * ngz * per + m, ngz, stride=per)
            total = out[rows, :]
            for f in range(2):
                start = 2 * cz + cx * f
                piece = pltpu.roll(tz[f][:, c * LANES : (c + 1) * LANES], (start - low) % LANES, 1)
                total = jnp.where((lane8 >= start) & (lane8 < start + cx), piece, total)
            out[rows, :] = total


def backward_kernel(
    u_hbm, v_hbm, w_hbm, ul, uh, wl, wh, got, modes_hbm, sa, ca, sb, cb, sx, sz, eth, etl, mux, mum,
    pressure_hbm, u_out, v_out, w_out, sh, sl, kh, kl, fh, fl, ring, plow, phigh,
    u, v, w, modes, pressure, u_new, v_new, w_new, in_sem, p_sem, out_sem,
):
    cx, cz, ny = u.shape
    cells = cx * cz
    arrive = arrivals([(modes_hbm, modes), (u_hbm, u), (v_hbm, v), (w_hbm, w)], in_sem)
    fill_sine((sa, ca, sb, cb), sh, sl)
    fill_local(sx, sz, kh, kl)

    arrive[0].wait()

    @pl.loop(0, ny // TILE)
    def _(n):
        cols = pl.ds(pl.multiple_of(n * TILE, TILE), TILE)
        edge = split(got[cols, :].T)
        field = dot3((eth[...], etl[...]), edge) - modes[:, cols]
        field = field / (mux[...] + mum[:, cols])
        field = split(by_parity(kh, kl, field))
        fh[:cells, cols], fl[:cells, cols] = field
        fh[cells:, cols], fl[cells:, cols] = edge

    @pl.loop(0, ny // TILE)
    def _(n):
        cols = pl.ds(pl.multiple_of(n * TILE, TILE), TILE)
        wide = dot3((fh[...], fl[...]), (sh[:, cols], sl[:, cols]))
        even = wide[: cells // 2].reshape(cx // 2, cz, TILE)
        odd = wide[cells // 2 : cells].reshape(cx // 2, cz, TILE)
        pressure[: cx // 2, :, cols] = even + odd
        for x in range(cx // 2):
            pressure[cx - 1 - x, :, cols] = even[x] - odd[x]
        ring[:, cols] = wide[cells:]

        @pl.when(n > 0)
        def _():
            tile_copy(pressure, pressure_hbm, p_sem, n - 1).start()

    for c in arrive[1:]:
        c.wait()

    plow[...] = ring[:cz, :] - 0.5 * ul[...].astype(F32)
    phigh[...] = ring[cz : 2 * cz, :] + 0.5 * uh[...].astype(F32)
    edge = pl.ds(2 * cz, cx)
    ring[edge, :] = ring[edge, :] - 0.5 * wl[...].astype(F32)
    edge = pl.ds(2 * cz + cx, cx)
    ring[edge, :] = ring[edge, :] + 0.5 * wh[...].astype(F32)

    def finish(x, before, after):
        here = pressure[x]
        u_new[x] = u[x].astype(F32) - 0.5 * (after - before)
        v_new[x] = v[x].astype(F32) - 0.5 * along_lanes(here)
        first = ring[pl.ds(2 * cz + x, 1), :]
        last = ring[pl.ds(2 * cz + cx + x, 1), :]
        w_new[x] = w[x].astype(F32) - 0.5 * along_rows(here, first, last)

    def leave(x):
        planes = [(u_new, u_out), (v_new, v_out), (w_new, w_out)]
        return [
            pltpu.make_async_copy(a.at[x], b.at[x], out_sem.at[i, x])
            for i, (a, b) in enumerate(planes)
        ]

    finish(0, plow[...], pressure[1])
    finish(cx - 1, pressure[cx - 2], phigh[...])
    tile_copy(pressure, pressure_hbm, p_sem, ny // TILE - 1).start()

    @pl.loop(1, cx - 1)
    def _(x):
        finish(x, pressure[x - 1], pressure[x + 1])
        for c in leave(x - 1):
            c.start()

    for x in (cx - 1, cx - 2):
        for c in leave(x):
            c.start()

    @pl.loop(0, ny // TILE)
    def _(n):
        tile_copy(pressure, pressure_hbm, p_sem, n).wait()

    @pl.loop(0, cx)
    def _(x):
        for c in leave(x):
            c.wait()


def _(x):
        finish(x, pressure[x - 1], pressure[x + 1])


def shifted(block, axis, step):
    count = lax.axis_size(axis)
    return lax.ppermute(block, axis, [(i, (i + step) % count) for i in range(count)])


def call(kernel, name, outs, scratch, flops, *args, places=(), out_places=()):
    spaces, out_spaces = dict(places), dict(out_places)
    size = sum(math.prod(a.shape) * a.dtype.itemsize for a in [*args, *outs])
    return pl.pallas_call(
        kernel,
        out_shape=outs,
        in_specs=[
            pl.BlockSpec(memory_space=spaces.get(i, pltpu.VMEM)) for i in range(len(args))
        ],
        out_specs=[
            pl.BlockSpec(memory_space=out_spaces.get(i, pltpu.VMEM)) for i in range(len(outs))
        ],
        scratch_shapes=scratch,
        compiler_params=pltpu.CompilerParams(vmem_limit_bytes=60 << 20),
        cost_estimate=pl.CostEstimate(flops=flops, bytes_accessed=size, transcendentals=0),
        name=name,
    )(*args)


def on_device(u_vel, v_vel, w_vel):
    cx, cz, ny = u_vel.shape
    ngx = lax.axis_size("gx")
    ngz = lax.axis_size("gz")
    nx, nz = ngx * cx, ngz * cz
    devices = ngx * ngz
    per = ny // devices
    cells = cx * cz
    edges = 2 * (cx + cz)
    me = lax.axis_index("gx") * ngz + lax.axis_index("gz")
    u_low = shifted(u_vel[-1], "gx", 1)
    u_high = shifted(u_vel[0], "gx", -1)
    w_low = shifted(w_vel[:, -1], "gz", 1)
    w_high = shifted(w_vel[:, 0], "gz", -1)
    sine_x = sine_np(cx)
    parity = np.arange(cx).reshape(cx // 2, 2).T
    order = parity.reshape(-1)
    local = np.kron(sine_x[:, order], sine_np(cz))[edge_rows(cx, cz)]
    tables = [f32(t) for t in sine_parts_np(ny, 32)]
    near = sine_x[: cx // 2]
    to_modes = np.repeat(near[:, order].T, cz, 1)
    to_cells = np.repeat(np.concatenate([near[:, p] for p in parity]), cz, 1)
    along_z = f32(np.tile(sine_np(cz), (1, cx // 2)))
    mux = f32(np.add.outer(wall_eigen_np(cx)[order], wall_eigen_np(cz)).reshape(-1, 1))
    mum = f32(wall_eigen_np(ny).reshape(1, -1))
    shape = jax.ShapeDtypeStruct
    square = [pltpu.VMEM((ny, ny), BF16)] * 2 + [pltpu.VMEM((cells, cells // 2), BF16)] * 2
    planes = [pltpu.VMEM((cx, cz, ny), BF16)] * 3
    send, modes = call(
        forward_kernel,
        "forward",
        [shape((ny, edges), F32), shape((cells, ny), F32)],
        square
        + [pltpu.VMEM((cells + edges, ny), BF16), pltpu.VMEM((cells, ny), BF16)]
        + planes
        + [pltpu.VMEM((cells, ny), F32)]
        + [pltpu.SemaphoreType.DMA((3,)), pltpu.SemaphoreType.DMA((ny // TILE,))],
        6 * cells * ny * (ny + cells + edges),
        u_vel, v_vel, w_vel, *tables, f32(to_modes), along_z, *halves(local), mux, mum,
        places={i: pl.ANY for i in range(3)},
        out_places={1: pl.ANY},
    )
    send = send.reshape(devices, per, 1, edges)
    seen = lax.all_to_all(send, ("gx", "gz"), split_axis=0, concat_axis=0, tiled=True)
    hx, hz = hartley_np(nx), hartley_np(nz)
    block_x, block_z = np.arange(ngx) * cx, np.arange(ngz) * cz
    lx = hx[:, np.concatenate([(block_x - 1) % nx, (block_x + cx) % nx])]
    lz = hz[:, np.concatenate([(block_z - 1) % nz, (block_z + cz) % nz])]
    lam_m = lax.dynamic_slice(jnp.asarray(mum[0]), (me * per,), (per,))
    (back,) = call(
        functools.partial(owner_kernel, ngx, ngz, cx, cz),
        "owner",
        [shape((ny, edges), F32)],
        [],
        6 * per * nx * nz * 200,
        seen.reshape(ny, edges),
        *halves(hx), *halves(hz), *halves(lx), *halves(lx.T), *halves(lz.T),
        f32(periodic_eigen_np(nz).reshape(1, -1)),
        f32(periodic_eigen_np(nx).reshape(-1, 1)),
        jnp.broadcast_to(lam_m[:, None], (per, LANES)),
    )
    back = back.reshape(devices, per, 1, edges)
    got = lax.all_to_all(back, ("gx", "gz"), split_axis=0, concat_axis=0, tiled=True)
    block = shape((cx, cz, ny), F32)
    return tuple(
        call(
            backward_kernel,
            "backward",
            [block] * 4,
            square
            + [pltpu.VMEM((cells + edges, ny), BF16)] * 2
            + [pltpu.VMEM((edges, ny), F32)]
            + [pltpu.VMEM((cz, ny), F32)] * 2
            + planes
            + [pltpu.VMEM((cells, ny), F32)]
            + [pltpu.VMEM((cx, cz, ny), F32)] * 4
            + [pltpu.SemaphoreType.DMA((4,)), pltpu.SemaphoreType.DMA((ny // TILE,))]
            + [pltpu.SemaphoreType.DMA((3, cx))],
            6 * cells * ny * (ny + cells + edges),
            u_vel, v_vel, w_vel, u_low, u_high, w_low, w_high, got.reshape(ny, edges), modes,
            *tables, f32(to_cells), along_z, *halves(local.T), mux, mum,
            places={i: pl.ANY for i in (0, 1, 2, 8)},
            out_places={i: pl.ANY for i in range(4)},
        )
    )


def solution(mesh):
    spec = P("gx", "gz", None)
    return jax.shard_map(
        on_device, mesh=mesh, in_specs=(spec,) * 3, out_specs=(spec,) * 4, check_vma=False
    )
```

```python
import functools
import math

import jax
import jax.numpy as jnp
import numpy as np
from jax import lax
from jax.experimental import pallas as pl
from jax.experimental.pallas import tpu as pltpu
from jax.sharding import PartitionSpec as P

F32 = jnp.float32
BF16 = jnp.bfloat16
TILE = 256
LANES = 128


def hartley_np(count):
    index = np.arange(count)
    angle = (index[:, None] * index[None, :] % count) * (2.0 * np.pi / count)
    return np.cos(angle) + np.sin(angle)


def sine_np(count):
    index = np.arange(1, count + 1)
    angle = (index[:, None] * index[None, :] % (2 * (count + 1))) * (np.pi / (count + 1))
    return np.sqrt(2.0 / (count + 1)) * np.sin(angle)


def sine_parts_np(count, step):
    mode = np.arange(1, count + 1)
    coarse = np.arange(0, count, step)
    fine = np.arange(1, step + 1)
    size = np.sqrt(2.0 / (count + 1))
    angle_c = (coarse[:, None] * mode % (2 * (count + 1))) * (np.pi / (count + 1))
    angle_f = (fine[:, None] * mode % (2 * (count + 1))) * (np.pi / (count + 1))
    return (
        size * np.sin(angle_c),
        size * np.cos(angle_c),
        np.sin(angle_f),
        np.cos(angle_f),
    )


def wall_eigen_np(count):
    return 4.0 * np.sin(np.arange(1, count + 1) * (np.pi / (2 * count + 2))) ** 2


def periodic_eigen_np(count):
    return 4.0 * np.sin(np.arange(count) * (np.pi / count)) ** 2


def edge_rows(cx, cz):
    grid = np.arange(cx * cz).reshape(cx, cz)
    return np.concatenate([grid[0], grid[-1], grid[:, 0], grid[:, -1]])


def f32(array):
    return np.ascontiguousarray(np.asarray(array, np.float32))


def halves(array):
    array = np.asarray(array, np.float32)
    high = array.astype(BF16)
    low = (array - high.astype(np.float32)).astype(BF16)
    return [high, low]


def split(x):
    high = x.astype(BF16)
    return high, (x - high.astype(F32)).astype(BF16)


def dot(a, b):
    return jnp.dot(a, b, preferred_element_type=F32)


def dot_t(a, b):
    return lax.dot_general(a, b, (((1,), (1,)), ((), ())), preferred_element_type=F32)


def dot3(a, b, op=dot):
    return op(a[0], b[0]) + op(a[1], b[0]) + op(a[0], b[1])


def fill_sine(parts, high, low):
    sa, ca, sb, cb = parts
    step = sb.shape[0]

    @pl.loop(0, sa.shape[0])
    def _(a):
        block = sa[pl.ds(a, 1), :] * cb[...] + ca[pl.ds(a, 1), :] * sb[...]
        rows = pl.ds(pl.multiple_of(a * step, step), step)
        high[rows, :], low[rows, :] = split(block)


def fill_local(sx, sz, high, low):
    step = sz.shape[0]

    @pl.loop(0, sx.shape[0])
    def _(a):
        rows = pl.ds(pl.multiple_of(a * step, step), step)
        high[rows, :], low[rows, :] = split(sx[pl.ds(a, 1), :] * sz[...])


def by_parity(high, low, field):
    half = field.shape[0] // 2
    parts = []
    for part in (slice(0, half), slice(half, 2 * half)):
        parts.append(dot3((high[part, :], low[part, :]), split(field[part])))
    return jnp.concatenate(parts, 0)


def along_rows(x, first, last):
    rows = x.shape[0]
    at = lax.broadcasted_iota(jnp.int32, x.shape, 0)
    up = jnp.where(at == rows - 1, last, pltpu.roll(x, rows - 1, 0))
    down = jnp.where(at == 0, first, pltpu.roll(x, 1, 0))
    return up - down


def along_lanes(x):
    lanes = x.shape[1]
    at = lax.broadcasted_iota(jnp.int32, x.shape, 1)
    up = jnp.where(at == lanes - 1, 0.0, pltpu.roll(x, lanes - 1, 1))
    down = jnp.where(at == 0, 0.0, pltpu.roll(x, 1, 1))
    return up - down


def arrivals(pairs, sems):
    copies = [pltpu.make_async_copy(a, b, sems.at[i]) for i, (a, b) in enumerate(pairs)]
    for c in copies:
        c.start()
    return copies


def tile_copy(source, target, sems, n):
    cols = pl.ds(pl.multiple_of(n * TILE, TILE), TILE)
    return pltpu.make_async_copy(source.at[..., cols], target.at[..., cols], sems.at[n])


def forward_kernel(
    u_hbm, v_hbm, w_hbm, sa, ca, sb, cb, sx, sz, eh, el, mux, mum, send, modes_hbm,
    sh, sl, kh, kl, dh, dl, u, v, w, modes, in_sem, out_sem,
):
    cx, cz, ny = u.shape
    cells = cx * cz
    arrive = arrivals([(u_hbm, u), (v_hbm, v), (w_hbm, w)], in_sem)
    fill_sine((sa, ca, sb, cb), sh, sl)
    fill_local(sx, sz, kh, kl)
    for c in arrive:
        c.wait()

    def divergence(x):
        after = u[jnp.minimum(x + 1, cx - 1)].astype(F32) * jnp.where(x < cx - 1, 1.0, 0.0)
        before = u[jnp.maximum(x - 1, 0)].astype(F32) * jnp.where(x > 0, 1.0, 0.0)
        return 0.5 * (
            (after - before)
            + along_lanes(v[x].astype(F32))
            + along_rows(w[x].astype(F32), 0.0, 0.0)
        )

    @pl.loop(0, cx // 2)
    def _(x):
        left, right = divergence(x), divergence(cx - 1 - x)
        rows = pl.ds(pl.multiple_of(x * cz, cz), cz)
        dh[rows, :], dl[rows, :] = split(left + right)
        rows = pl.ds(pl.multiple_of(cells // 2 + x * cz, cz), cz)
        dh[rows, :], dl[rows, :] = split(left - right)

    dh[cells : cells + cz, :] = (-0.5 * u[0].astype(F32)).astype(BF16)
    dh[cells + cz : cells + 2 * cz, :] = (0.5 * u[cx - 1].astype(F32)).astype(BF16)
    dh[cells + 2 * cz : cells + 2 * cz + cx, :] = (-0.5 * w[:, 0, :].astype(F32)).astype(BF16)
    dh[cells + 2 * cz + cx :, :] = (0.5 * w[:, cz - 1, :].astype(F32)).astype(BF16)

    @pl.loop(0, ny // TILE)
    def _(n):
        cols = pl.ds(pl.multiple_of(n * TILE, TILE), TILE)
        wide = dot(dh[...], sh[:, cols]) + dot(dh[...], sl[:, cols])
        field = wide[:cells] + dot(dl[...], sh[:, cols])
        mode = by_parity(kh, kl, field)
        modes[:, cols] = mode
        mode = mode / (mux[...] + mum[:, cols])
        edge = wide[cells:] - dot3((eh[...], el[...]), split(mode))
        send[cols, :] = edge.T
        tile_copy(modes, modes_hbm, out_sem, n).start()

    @pl.loop(0, ny // TILE)
    def _(n):
        tile_copy(modes, modes_hbm, out_sem, n).wait()


def owner_kernel(
    ngx, ngz, cx, cz, seen, hxh, hxl, hzh, hzl, lxh, lxl, lxth, lxtl, lzth, lztl, muz, mukx, mum, out
):
    per = mum.shape[0] // (ngx * ngz)
    me = lax.axis_index("gx") * ngz + lax.axis_index("gz")
    nx, nz = ngx * cx, ngz * cz
    lane = lax.broadcasted_iota(jnp.int32, (ngx, LANES), 1)
    lane8 = lax.broadcasted_iota(jnp.int32, (ngz, LANES), 1)
    wide_x = nz // LANES
    wide_z = nx // LANES
    hx = (hxh[...], hxl[...])
    hz = (hzh[...], hzl[...])
    px, pz = [], []
    for m in range(per):
        cols = [[jnp.zeros((ngx, LANES), F32)] * wide_x for _ in range(2)]
        for j in range(ngz):
            piece = seen[pl.ds(j * per + m, ngx, stride=ngz * per), :]
            for f in range(2):
                turned = pltpu.roll(piece, (cz * j - cz * f) % LANES, 1)
                for c in range(wide_x):
                    low, high = cz * j - c * LANES, cz * (j + 1) - c * LANES
                    if high > 0 and low < LANES:
                        cols[f][c] = jnp.where((lane >= low) & (lane < high), turned, cols[f][c])
        px += [jnp.concatenate(c, 1) for c in cols]
        cols = [[jnp.zeros((ngz, LANES), F32)] * wide_z for _ in range(2)]
        for i in range(ngx):
            piece = seen[pl.ds(i * ngz * per + m, ngz, stride=per), :]
            c, low = cx * i // LANES, cx * i % LANES
            for f in range(2):
                turned = pltpu.roll(piece, (low - 2 * cz - cx * f) % LANES, 1)
                cols[f][c] = jnp.where((lane8 >= low) & (lane8 < low + cx), turned, cols[f][c])
        pz += [jnp.concatenate(c, 1) for c in cols]
    f1 = dot3(split(jnp.concatenate(px, 0)), hz)
    f2 = dot3(split(jnp.concatenate(pz, 0)), hx)
    ex, ez = [], []
    for m in range(per):
        mine = f1[2 * ngx * m : 2 * ngx * (m + 1)]
        other = f2[2 * ngz * m : 2 * ngz * (m + 1)].T
        spec = dot3((lxh[...], lxl[...]), split(mine)) + dot3(split(other), (lzth[...], lztl[...]))
        spec = spec / ((mukx[...] + muz[...] + mum[me * per + m]) * (-float(nx * nz)))
        spec = split(spec)
        ex.append(dot3((lxth[...], lxtl[...]), spec))
        ez.append(dot3((lzth[...], lztl[...]), spec, dot_t))
    ex = -dot3(split(jnp.concatenate(ex, 0)), hz)
    ez = -dot3(split(jnp.concatenate(ez, 0)), hx)
    for m in range(per):
        tx, tz = [], []
        for f in range(2):
            at = 2 * ngx * m + f * ngx
            turn = 1 if f == 0 else ngx - 1
            tx.append(ex[at : at + ngx] + pltpu.roll(px[2 * m + 1 - f], turn, 0))
            at = 2 * ngz * m + f * ngz
            turn = 1 if f == 0 else ngz - 1
            tz.append(ez[at : at + ngz] + pltpu.roll(pz[2 * m + 1 - f], turn, 0))
        for j in range(ngz):
            c, low = cz * j // LANES, cz * j % LANES
            total = jnp.zeros((ngx, LANES), F32)
            for f in range(2):
                piece = tx[f][:, c * LANES : (c + 1) * LANES]
                if low + cz > LANES:
                    after = tx[f][:, (c + 1) * LANES : (c + 2) * LANES]
                    piece = jnp.where(lane >= low, piece, after)
                piece = pltpu.roll(piece, (cz * f - low) % LANES, 1)
                total = jnp.where((lane >= cz * f) & (lane < cz * (f + 1)), piece, total)
            out[pl.ds(j * per + m, ngx, stride=ngz * per), :] = total
        for i in range(ngx):
            c, low = cx * i // LANES, cx * i % LANES
            rows = pl.ds(i * ngz * per + m, ngz, stride=per)
            total = out[rows, :]
            for f in range(2):
                start = 2 * cz + cx * f
                piece = pltpu.roll(tz[f][:, c * LANES : (c + 1) * LANES], (start - low) % LANES, 1)
                total = jnp.where((lane8 >= start) & (lane8 < start + cx), piece, total)
            out[rows, :] = total


def backward_kernel(
    u_hbm, v_hbm, w_hbm, ul, uh, wl, wh, got, modes_hbm, sa, ca, sb, cb, sx, sz, eth, etl, mux, mum,
    pressure_hbm, u_out, v_out, w_out, sh, sl, kh, kl, fh, fl, ring, plow, phigh,
    u, v, w, modes, pressure, u_new, v_new, w_new, in_sem, p_sem, out_sem,
):
    cx, cz, ny = u.shape
    cells = cx * cz
    arrive = arrivals([(modes_hbm, modes), (u_hbm, u), (v_hbm, v), (w_hbm, w)], in_sem)
    fill_sine((sa, ca, sb, cb), sh, sl)
    fill_local(sx, sz, kh, kl)

    arrive[0].wait()

    @pl.loop(0, ny // TILE)
    def _(n):
        cols = pl.ds(pl.multiple_of(n * TILE, TILE), TILE)
        edge = split(got[cols, :].T)
        field = dot3((eth[...], etl[...]), edge) - modes[:, cols]
        field = field / (mux[...] + mum[:, cols])
        field = split(by_parity(kh, kl, field))
        fh[:cells, cols], fl[:cells, cols] = field
        fh[cells:, cols], fl[cells:, cols] = edge

    @pl.loop(0, ny // TILE)
    def _(n):
        cols = pl.ds(pl.multiple_of(n * TILE, TILE), TILE)
        wide = dot3((fh[...], fl[...]), (sh[:, cols], sl[:, cols]))
        even = wide[: cells // 2].reshape(cx // 2, cz, TILE)
        odd = wide[cells // 2 : cells].reshape(cx // 2, cz, TILE)
        pressure[: cx // 2, :, cols] = even + odd
        for x in range(cx // 2):
            pressure[cx - 1 - x, :, cols] = even[x] - odd[x]
        ring[:, cols] = wide[cells:]

        @pl.when(n > 0)
        def _():
            tile_copy(pressure, pressure_hbm, p_sem, n - 1).start()

    for c in arrive[1:]:
        c.wait()

    plow[...] = ring[:cz, :] - 0.5 * ul[...].astype(F32)
    phigh[...] = ring[cz : 2 * cz, :] + 0.5 * uh[...].astype(F32)
    edge = pl.ds(2 * cz, cx)
    ring[edge, :] = ring[edge, :] - 0.5 * wl[...].astype(F32)
    edge = pl.ds(2 * cz + cx, cx)
    ring[edge, :] = ring[edge, :] + 0.5 * wh[...].astype(F32)

    def finish(x, before, after):
        here = pressure[x]
        u_new[x] = u[x].astype(F32) - 0.5 * (after - before)
        v_new[x] = v[x].astype(F32) - 0.5 * along_lanes(here)
        first = ring[pl.ds(2 * cz + x, 1), :]
        last = ring[pl.ds(2 * cz + cx + x, 1), :]
        w_new[x] = w[x].astype(F32) - 0.5 * along_rows(here, first, last)

    def leave(x):
        planes = [(u_new, u_out), (v_new, v_out), (w_new, w_out)]
        return [
            pltpu.make_async_copy(a.at[x], b.at[x], out_sem.at[i, x])
            for i, (a, b) in enumerate(planes)
        ]

    finish(0, plow[...], pressure[1])
    finish(cx - 1, pressure[cx - 2], phigh[...])
    tile_copy(pressure, pressure_hbm, p_sem, ny // TILE - 1).start()

    @pl.loop(1, cx - 1)
    def _(x):
        finish(x, pressure[x - 1], pressure[x + 1])
        for c in leave(x - 1):
            c.start()

    for x in (cx - 1, cx - 2):
        for c in leave(x):
            c.start()

    @pl.loop(0, ny // TILE)
    def _(n):
        tile_copy(pressure, pressure_hbm, p_sem, n).wait()

    @pl.loop(0, cx)
    def _(x):
        for c in leave(x):
            c.wait()


def _(x):
        finish(x, pressure[x - 1], pressure[x + 1])


def shifted(block, axis, step):
    count = lax.axis_size(axis)
    return lax.ppermute(block, axis, [(i, (i + step) % count) for i in range(count)])


def call(kernel, name, outs, scratch, flops, *args, places=(), out_places=(), vmem=60 << 20):
    spaces, out_spaces = dict(places), dict(out_places)
    size = sum(math.prod(a.shape) * a.dtype.itemsize for a in [*args, *outs])
    return pl.pallas_call(
        kernel,
        out_shape=outs,
        in_specs=[
            pl.BlockSpec(memory_space=spaces.get(i, pltpu.VMEM)) for i in range(len(args))
        ],
        out_specs=[
            pl.BlockSpec(memory_space=out_spaces.get(i, pltpu.VMEM)) for i in range(len(outs))
        ],
        scratch_shapes=scratch,
        compiler_params=pltpu.CompilerParams(vmem_limit_bytes=vmem),
        cost_estimate=pl.CostEstimate(flops=flops, bytes_accessed=size, transcendentals=0),
        name=name,
    )(*args)


def on_device(u_vel, v_vel, w_vel):
    cx, cz, ny = u_vel.shape
    ngx = lax.axis_size("gx")
    ngz = lax.axis_size("gz")
    nx, nz = ngx * cx, ngz * cz
    devices = ngx * ngz
    per = ny // devices
    cells = cx * cz
    edges = 2 * (cx + cz)
    u_low = shifted(u_vel[-1], "gx", 1)
    u_high = shifted(u_vel[0], "gx", -1)
    w_low = shifted(w_vel[:, -1], "gz", 1)
    w_high = shifted(w_vel[:, 0], "gz", -1)
    sine_x = sine_np(cx)
    parity = np.arange(cx).reshape(cx // 2, 2).T
    order = parity.reshape(-1)
    local = np.kron(sine_x[:, order], sine_np(cz))[edge_rows(cx, cz)]
    tables = [f32(t) for t in sine_parts_np(ny, 32)]
    near = sine_x[: cx // 2]
    to_modes = np.repeat(near[:, order].T, cz, 1)
    to_cells = np.repeat(np.concatenate([near[:, p] for p in parity]), cz, 1)
    along_z = f32(np.tile(sine_np(cz), (1, cx // 2)))
    mux = f32(np.add.outer(wall_eigen_np(cx)[order], wall_eigen_np(cz)).reshape(-1, 1))
    mum = f32(wall_eigen_np(ny).reshape(1, -1))
    shape = jax.ShapeDtypeStruct
    square = [pltpu.VMEM((ny, ny), BF16)] * 2 + [pltpu.VMEM((cells, cells // 2), BF16)] * 2
    planes = [pltpu.VMEM((cx, cz, ny), BF16)] * 3
    send, modes = call(
        forward_kernel,
        "forward",
        [shape((ny, edges), F32), shape((cells, ny), F32)],
        square
        + [pltpu.VMEM((cells + edges, ny), BF16), pltpu.VMEM((cells, ny), BF16)]
        + planes
        + [pltpu.VMEM((cells, ny), F32)]
        + [pltpu.SemaphoreType.DMA((3,)), pltpu.SemaphoreType.DMA((ny // TILE,))],
        6 * cells * ny * (ny + cells + edges),
        u_vel, v_vel, w_vel, *tables, f32(to_modes), along_z, *halves(local), mux, mum,
        places={i: pl.ANY for i in range(3)},
        out_places={1: pl.ANY},
    )
    send = send.reshape(devices, per, 1, edges)
    seen = lax.all_to_all(send, ("gx", "gz"), split_axis=0, concat_axis=0, tiled=True)
    hx, hz = hartley_np(nx), hartley_np(nz)
    block_x, block_z = np.arange(ngx) * cx, np.arange(ngz) * cz
    lx = hx[:, np.concatenate([(block_x - 1) % nx, (block_x + cx) % nx])]
    lz = hz[:, np.concatenate([(block_z - 1) % nz, (block_z + cz) % nz])]
    (back,) = call(
        functools.partial(owner_kernel, ngx, ngz, cx, cz),
        "owner",
        [shape((ny, edges), F32)],
        [],
        6 * per * nx * nz * 200,
        seen.reshape(ny, edges),
        *halves(hx), *halves(hz), *halves(lx), *halves(lx.T), *halves(lz.T),
        f32(periodic_eigen_np(nz).reshape(1, -1)),
        f32(periodic_eigen_np(nx).reshape(-1, 1)),
        f32(mum[0]),
        places={13: pltpu.SMEM},
        vmem=20 << 20,
    )
    back = back.reshape(devices, per, 1, edges)
    got = lax.all_to_all(back, ("gx", "gz"), split_axis=0, concat_axis=0, tiled=True)
    block = shape((cx, cz, ny), F32)
    return tuple(
        call(
            backward_kernel,
            "backward",
            [block] * 4,
            square
            + [pltpu.VMEM((cells + edges, ny), BF16)] * 2
            + [pltpu.VMEM((edges, ny), F32)]
            + [pltpu.VMEM((cz, ny), F32)] * 2
            + planes
            + [pltpu.VMEM((cells, ny), F32)]
            + [pltpu.VMEM((cx, cz, ny), F32)] * 4
            + [pltpu.SemaphoreType.DMA((4,)), pltpu.SemaphoreType.DMA((ny // TILE,))]
            + [pltpu.SemaphoreType.DMA((3, cx))],
            6 * cells * ny * (ny + cells + edges),
            u_vel, v_vel, w_vel, u_low, u_high, w_low, w_high, got.reshape(ny, edges), modes,
            *tables, f32(to_cells), along_z, *halves(local.T), mux, mum,
            places={i: pl.ANY for i in (0, 1, 2, 8)},
            out_places={i: pl.ANY for i in range(4)},
            vmem=60 << 20,
        )
    )


def solution(mesh):
    spec = P("gx", "gz", None)
    return jax.shard_map(
        on_device, mesh=mesh, in_specs=(spec,) * 3, out_specs=(spec,) * 4, check_vma=False
    )
```

```python
import functools
import math

import jax
import jax.numpy as jnp
import numpy as np
from jax import lax
from jax.experimental import pallas as pl
from jax.experimental.pallas import tpu as pltpu
from jax.sharding import PartitionSpec as P

F32 = jnp.float32
BF16 = jnp.bfloat16
TILE = 256
LANES = 128


def hartley_np(count):
    index = np.arange(count)
    angle = (index[:, None] * index[None, :] % count) * (2.0 * np.pi / count)
    return np.cos(angle) + np.sin(angle)


def sine_np(count):
    index = np.arange(1, count + 1)
    angle = (index[:, None] * index[None, :] % (2 * (count + 1))) * (np.pi / (count + 1))
    return np.sqrt(2.0 / (count + 1)) * np.sin(angle)


def sine_parts_np(count, step):
    mode = np.arange(1, count + 1)
    coarse = np.arange(0, count, step)
    fine = np.arange(1, step + 1)
    size = np.sqrt(2.0 / (count + 1))
    angle_c = (coarse[:, None] * mode % (2 * (count + 1))) * (np.pi / (count + 1))
    angle_f = (fine[:, None] * mode % (2 * (count + 1))) * (np.pi / (count + 1))
    return (
        size * np.sin(angle_c),
        size * np.cos(angle_c),
        np.sin(angle_f),
        np.cos(angle_f),
    )


def wall_eigen_np(count):
    return 4.0 * np.sin(np.arange(1, count + 1) * (np.pi / (2 * count + 2))) ** 2


def periodic_eigen_np(count):
    return 4.0 * np.sin(np.arange(count) * (np.pi / count)) ** 2


def edge_rows(cx, cz):
    grid = np.arange(cx * cz).reshape(cx, cz)
    return np.concatenate([grid[0], grid[-1], grid[:, 0], grid[:, -1]])


def f32(array):
    return np.ascontiguousarray(np.asarray(array, np.float32))


def halves(array):
    array = np.asarray(array, np.float32)
    high = array.astype(BF16)
    low = (array - high.astype(np.float32)).astype(BF16)
    return [high, low]


def split(x):
    high = x.astype(BF16)
    return high, (x - high.astype(F32)).astype(BF16)


def dot(a, b):
    return jnp.dot(a, b, preferred_element_type=F32)


def dot_t(a, b):
    return lax.dot_general(a, b, (((1,), (1,)), ((), ())), preferred_element_type=F32)


def dot3(a, b, op=dot):
    return op(a[0], b[0]) + op(a[1], b[0]) + op(a[0], b[1])


def fill_sine(parts, high, low):
    sa, ca, sb, cb = parts
    step = sb.shape[0]

    @pl.loop(0, sa.shape[0])
    def _(a):
        block = sa[pl.ds(a, 1), :] * cb[...] + ca[pl.ds(a, 1), :] * sb[...]
        rows = pl.ds(pl.multiple_of(a * step, step), step)
        high[rows, :], low[rows, :] = split(block)


def fill_local(sx, sz, high, low):
    step = sz.shape[0]

    @pl.loop(0, sx.shape[0])
    def _(a):
        rows = pl.ds(pl.multiple_of(a * step, step), step)
        high[rows, :], low[rows, :] = split(sx[pl.ds(a, 1), :] * sz[...])


def by_parity(high, low, field):
    half = field.shape[0] // 2
    parts = []
    for part in (slice(0, half), slice(half, 2 * half)):
        parts.append(dot3((high[part, :], low[part, :]), split(field[part])))
    return jnp.concatenate(parts, 0)


def along_rows(x, first, last):
    rows = x.shape[0]
    at = lax.broadcasted_iota(jnp.int32, x.shape, 0)
    up = jnp.where(at == rows - 1, last, pltpu.roll(x, rows - 1, 0))
    down = jnp.where(at == 0, first, pltpu.roll(x, 1, 0))
    return up - down


def along_lanes(x):
    lanes = x.shape[1]
    at = lax.broadcasted_iota(jnp.int32, x.shape, 1)
    up = jnp.where(at == lanes - 1, 0.0, pltpu.roll(x, lanes - 1, 1))
    down = jnp.where(at == 0, 0.0, pltpu.roll(x, 1, 1))
    return up - down


def arrivals(pairs, sems):
    copies = [pltpu.make_async_copy(a, b, sems.at[i]) for i, (a, b) in enumerate(pairs)]
    for c in copies:
        c.start()
    return copies


def tile_copy(source, target, sems, n):
    cols = pl.ds(pl.multiple_of(n * TILE, TILE), TILE)
    return pltpu.make_async_copy(source.at[..., cols], target.at[..., cols], sems.at[n])


def forward_kernel(
    u_hbm, v_hbm, w_hbm, sa, ca, sb, cb, sx, sz, eh, el, mux, mum, send, modes_hbm,
    sh, sl, kh, kl, dh, dl, u, v, w, modes, in_sem, out_sem,
):
    cx, cz, ny = u.shape
    cells = cx * cz
    arrive = arrivals([(u_hbm, u), (v_hbm, v), (w_hbm, w)], in_sem)
    fill_sine((sa, ca, sb, cb), sh, sl)
    fill_local(sx, sz, kh, kl)
    for c in arrive:
        c.wait()

    def divergence(x):
        after = u[jnp.minimum(x + 1, cx - 1)].astype(F32) * jnp.where(x < cx - 1, 1.0, 0.0)
        before = u[jnp.maximum(x - 1, 0)].astype(F32) * jnp.where(x > 0, 1.0, 0.0)
        return 0.5 * (
            (after - before)
            + along_lanes(v[x].astype(F32))
            + along_rows(w[x].astype(F32), 0.0, 0.0)
        )

    @pl.loop(0, cx // 2)
    def _(x):
        left, right = divergence(x), divergence(cx - 1 - x)
        rows = pl.ds(pl.multiple_of(x * cz, cz), cz)
        dh[rows, :], dl[rows, :] = split(left + right)
        rows = pl.ds(pl.multiple_of(cells // 2 + x * cz, cz), cz)
        dh[rows, :], dl[rows, :] = split(left - right)

    dh[cells : cells + cz, :] = (-0.5 * u[0].astype(F32)).astype(BF16)
    dh[cells + cz : cells + 2 * cz, :] = (0.5 * u[cx - 1].astype(F32)).astype(BF16)
    dh[cells + 2 * cz : cells + 2 * cz + cx, :] = (-0.5 * w[:, 0, :].astype(F32)).astype(BF16)
    dh[cells + 2 * cz + cx :, :] = (0.5 * w[:, cz - 1, :].astype(F32)).astype(BF16)

    @pl.loop(0, ny // TILE)
    def _(n):
        cols = pl.ds(pl.multiple_of(n * TILE, TILE), TILE)
        wide = dot(dh[...], sh[:, cols]) + dot(dh[...], sl[:, cols])
        field = wide[:cells] + dot(dl[...], sh[:, cols])
        mode = by_parity(kh, kl, field)
        modes[:, cols] = mode
        mode = mode / (mux[...] + mum[:, cols])
        edge = wide[cells:] - dot3((eh[...], el[...]), split(mode))
        send[cols, :] = edge.T
        tile_copy(modes, modes_hbm, out_sem, n).start()

    @pl.loop(0, ny // TILE)
    def _(n):
        tile_copy(modes, modes_hbm, out_sem, n).wait()


def owner_kernel(
    ngx, ngz, cx, cz, seen, hxh, hxl, hzh, hzl, lxh, lxl, lxth, lxtl, lzth, lztl, muz, mukx, mum, out
):
    per = mum.shape[0] // (ngx * ngz)
    me = lax.axis_index("gx") * ngz + lax.axis_index("gz")
    nx, nz = ngx * cx, ngz * cz
    lane = lax.broadcasted_iota(jnp.int32, (ngx, LANES), 1)
    lane8 = lax.broadcasted_iota(jnp.int32, (ngz, LANES), 1)
    wide_x = nz // LANES
    wide_z = nx // LANES
    hx = (hxh[...], hxl[...])
    hz = (hzh[...], hzl[...])
    px, pz = [], []
    for m in range(per):
        cols = [[jnp.zeros((ngx, LANES), F32)] * wide_x for _ in range(2)]
        for j in range(ngz):
            piece = seen[pl.ds(j * per + m, ngx, stride=ngz * per), :]
            for f in range(2):
                turned = pltpu.roll(piece, (cz * j - cz * f) % LANES, 1)
                for c in range(wide_x):
                    low, high = cz * j - c * LANES, cz * (j + 1) - c * LANES
                    if high > 0 and low < LANES:
                        cols[f][c] = jnp.where((lane >= low) & (lane < high), turned, cols[f][c])
        px += [jnp.concatenate(c, 1) for c in cols]
        cols = [[jnp.zeros((ngz, LANES), F32)] * wide_z for _ in range(2)]
        for i in range(ngx):
            piece = seen[pl.ds(i * ngz * per + m, ngz, stride=per), :]
            c, low = cx * i // LANES, cx * i % LANES
            for f in range(2):
                turned = pltpu.roll(piece, (low - 2 * cz - cx * f) % LANES, 1)
                cols[f][c] = jnp.where((lane8 >= low) & (lane8 < low + cx), turned, cols[f][c])
        pz += [jnp.concatenate(c, 1) for c in cols]
    f1 = dot3(split(jnp.concatenate(px, 0)), hz)
    f2 = dot3(split(jnp.concatenate(pz, 0)), hx)
    ex, ez = [], []
    for m in range(per):
        mine = f1[2 * ngx * m : 2 * ngx * (m + 1)]
        other = f2[2 * ngz * m : 2 * ngz * (m + 1)].T
        spec = dot3((lxh[...], lxl[...]), split(mine)) + dot3(split(other), (lzth[...], lztl[...]))
        spec = spec / ((mukx[...] + muz[...] + mum[me * per + m]) * (-float(nx * nz)))
        spec = split(spec)
        ex.append(dot3((lxth[...], lxtl[...]), spec))
        ez.append(dot3((lzth[...], lztl[...]), spec, dot_t))
    ex = -dot3(split(jnp.concatenate(ex, 0)), hz)
    ez = -dot3(split(jnp.concatenate(ez, 0)), hx)
    for m in range(per):
        tx, tz = [], []
        for f in range(2):
            at = 2 * ngx * m + f * ngx
            turn = 1 if f == 0 else ngx - 1
            tx.append(ex[at : at + ngx] + pltpu.roll(px[2 * m + 1 - f], turn, 0))
            at = 2 * ngz * m + f * ngz
            turn = 1 if f == 0 else ngz - 1
            tz.append(ez[at : at + ngz] + pltpu.roll(pz[2 * m + 1 - f], turn, 0))
        for j in range(ngz):
            c, low = cz * j // LANES, cz * j % LANES
            total = jnp.zeros((ngx, LANES), F32)
            for f in range(2):
                piece = tx[f][:, c * LANES : (c + 1) * LANES]
                if low + cz > LANES:
                    after = tx[f][:, (c + 1) * LANES : (c + 2) * LANES]
                    piece = jnp.where(lane >= low, piece, after)
                piece = pltpu.roll(piece, (cz * f - low) % LANES, 1)
                total = jnp.where((lane >= cz * f) & (lane < cz * (f + 1)), piece, total)
            out[pl.ds(j * per + m, ngx, stride=ngz * per), :] = total
        for i in range(ngx):
            c, low = cx * i // LANES, cx * i % LANES
            rows = pl.ds(i * ngz * per + m, ngz, stride=per)
            total = out[rows, :]
            for f in range(2):
                start = 2 * cz + cx * f
                piece = pltpu.roll(tz[f][:, c * LANES : (c + 1) * LANES], (start - low) % LANES, 1)
                total = jnp.where((lane8 >= start) & (lane8 < start + cx), piece, total)
            out[rows, :] = total


def backward_kernel(
    u_hbm, v_hbm, w_hbm, ul, uh, wl, wh, got, modes_hbm, sa, ca, sb, cb, sx, sz, eth, etl, mux, mum,
    pressure_hbm, u_out, v_out, w_out, sh, sl, kh, kl, fh, fl, ring, plow, phigh,
    u, v, w, modes, pressure, u_new, v_new, w_new, in_sem, p_sem, out_sem,
):
    cx, cz, ny = u.shape
    cells = cx * cz
    arrive = arrivals([(modes_hbm, modes), (u_hbm, u), (v_hbm, v), (w_hbm, w)], in_sem)
    fill_sine((sa, ca, sb, cb), sh, sl)
    fill_local(sx, sz, kh, kl)

    arrive[0].wait()

    @pl.loop(0, ny // TILE)
    def _(n):
        cols = pl.ds(pl.multiple_of(n * TILE, TILE), TILE)
        edge = split(got[cols, :].T)
        field = dot3((eth[...], etl[...]), edge) - modes[:, cols]
        field = field / (mux[...] + mum[:, cols])
        field = split(by_parity(kh, kl, field))
        fh[:cells, cols], fl[:cells, cols] = field
        fh[cells:, cols], fl[cells:, cols] = edge

    @pl.loop(0, ny // TILE)
    def _(n):
        cols = pl.ds(pl.multiple_of(n * TILE, TILE), TILE)
        wide = dot3((fh[...], fl[...]), (sh[:, cols], sl[:, cols]))
        even = wide[: cells // 2].reshape(cx // 2, cz, TILE)
        odd = wide[cells // 2 : cells].reshape(cx // 2, cz, TILE)
        pressure[: cx // 2, :, cols] = even + odd
        for x in range(cx // 2):
            pressure[cx - 1 - x, :, cols] = even[x] - odd[x]
        ring[:, cols] = wide[cells:]

        @pl.when(n > 0)
        def _():
            tile_copy(pressure, pressure_hbm, p_sem, n - 1).start()

    for c in arrive[1:]:
        c.wait()

    plow[...] = ring[:cz, :] - 0.5 * ul[...].astype(F32)
    phigh[...] = ring[cz : 2 * cz, :] + 0.5 * uh[...].astype(F32)
    edge = pl.ds(2 * cz, cx)
    ring[edge, :] = ring[edge, :] - 0.5 * wl[...].astype(F32)
    edge = pl.ds(2 * cz + cx, cx)
    ring[edge, :] = ring[edge, :] + 0.5 * wh[...].astype(F32)

    def finish(x, before, after):
        here = pressure[x]
        u_new[x] = u[x].astype(F32) - 0.5 * (after - before)
        v_new[x] = v[x].astype(F32) - 0.5 * along_lanes(here)
        first = ring[pl.ds(2 * cz + x, 1), :]
        last = ring[pl.ds(2 * cz + cx + x, 1), :]
        w_new[x] = w[x].astype(F32) - 0.5 * along_rows(here, first, last)

    def leave(x):
        planes = [(u_new, u_out), (v_new, v_out), (w_new, w_out)]
        return [
            pltpu.make_async_copy(a.at[x], b.at[x], out_sem.at[i, x])
            for i, (a, b) in enumerate(planes)
        ]

    finish(0, plow[...], pressure[1])
    finish(cx - 1, pressure[cx - 2], phigh[...])
    tile_copy(pressure, pressure_hbm, p_sem, ny // TILE - 1).start()

    @pl.loop(1, cx - 1)
    def _(x):
        finish(x, pressure[x - 1], pressure[x + 1])
        for c in leave(x - 1):
            c.start()

    for x in (cx - 1, cx - 2):
        for c in leave(x):
            c.start()

    @pl.loop(0, ny // TILE)
    def _(n):
        tile_copy(pressure, pressure_hbm, p_sem, n).wait()

    @pl.loop(0, cx)
    def _(x):
        for c in leave(x):
            c.wait()


def _(x):
        finish(x, pressure[x - 1], pressure[x + 1])


def shifted(block, axis, step):
    count = lax.axis_size(axis)
    return lax.ppermute(block, axis, [(i, (i + step) % count) for i in range(count)])


def call(kernel, name, outs, scratch, flops, *args, places=(), out_places=(), vmem=60 << 20):
    spaces, out_spaces = dict(places), dict(out_places)
    size = sum(math.prod(a.shape) * a.dtype.itemsize for a in [*args, *outs])
    return pl.pallas_call(
        kernel,
        out_shape=outs,
        in_specs=[
            pl.BlockSpec(memory_space=spaces.get(i, pltpu.VMEM)) for i in range(len(args))
        ],
        out_specs=[
            pl.BlockSpec(memory_space=out_spaces.get(i, pltpu.VMEM)) for i in range(len(outs))
        ],
        scratch_shapes=scratch,
        compiler_params=pltpu.CompilerParams(vmem_limit_bytes=vmem),
        cost_estimate=pl.CostEstimate(flops=flops, bytes_accessed=size, transcendentals=0),
        name=name,
    )(*args)


def on_device(u_vel, v_vel, w_vel):
    cx, cz, ny = u_vel.shape
    ngx = lax.axis_size("gx")
    ngz = lax.axis_size("gz")
    nx, nz = ngx * cx, ngz * cz
    devices = ngx * ngz
    per = ny // devices
    cells = cx * cz
    edges = 2 * (cx + cz)
    u_low = shifted(u_vel[-1], "gx", 1)
    u_high = shifted(u_vel[0], "gx", -1)
    w_low = shifted(w_vel[:, -1], "gz", 1)
    w_high = shifted(w_vel[:, 0], "gz", -1)
    sine_x = sine_np(cx)
    parity = np.arange(cx).reshape(cx // 2, 2).T
    order = parity.reshape(-1)
    local = np.kron(sine_x[:, order], sine_np(cz))[edge_rows(cx, cz)]
    tables = [f32(t) for t in sine_parts_np(ny, 32)]
    near = sine_x[: cx // 2]
    to_modes = np.repeat(near[:, order].T, cz, 1)
    to_cells = np.repeat(np.concatenate([near[:, p] for p in parity]), cz, 1)
    along_z = f32(np.tile(sine_np(cz), (1, cx // 2)))
    mux = f32(np.add.outer(wall_eigen_np(cx)[order], wall_eigen_np(cz)).reshape(-1, 1))
    mum = f32(wall_eigen_np(ny).reshape(1, -1))
    shape = jax.ShapeDtypeStruct
    square = [pltpu.VMEM((ny, ny), BF16)] * 2 + [pltpu.VMEM((cells, cells // 2), BF16)] * 2
    planes = [pltpu.VMEM((cx, cz, ny), BF16)] * 3
    send, modes = call(
        forward_kernel,
        "forward",
        [shape((ny, edges), F32), shape((cells, ny), F32)],
        square
        + [pltpu.VMEM((cells + edges, ny), BF16), pltpu.VMEM((cells, ny), BF16)]
        + planes
        + [pltpu.VMEM((cells, ny), F32)]
        + [pltpu.SemaphoreType.DMA((3,)), pltpu.SemaphoreType.DMA((ny // TILE,))],
        6 * cells * ny * (ny + cells + edges),
        u_vel, v_vel, w_vel, *tables, f32(to_modes), along_z, *halves(local), mux, mum,
        places={i: pl.ANY for i in range(3)},
        out_places={1: pl.ANY},
    )
    send = send.reshape(devices, per, 1, edges)
    seen = lax.all_to_all(send, ("gx", "gz"), split_axis=0, concat_axis=0, tiled=True)
    seen, u_low, u_high, w_low, w_high = lax.optimization_barrier(
        (seen, u_low, u_high, w_low, w_high)
    )
    hx, hz = hartley_np(nx), hartley_np(nz)
    block_x, block_z = np.arange(ngx) * cx, np.arange(ngz) * cz
    lx = hx[:, np.concatenate([(block_x - 1) % nx, (block_x + cx) % nx])]
    lz = hz[:, np.concatenate([(block_z - 1) % nz, (block_z + cz) % nz])]
    (back,) = call(
        functools.partial(owner_kernel, ngx, ngz, cx, cz),
        "owner",
        [shape((ny, edges), F32)],
        [],
        6 * per * nx * nz * 200,
        seen.reshape(ny, edges),
        *halves(hx), *halves(hz), *halves(lx), *halves(lx.T), *halves(lz.T),
        f32(periodic_eigen_np(nz).reshape(1, -1)),
        f32(periodic_eigen_np(nx).reshape(-1, 1)),
        f32(mum[0]),
        places={13: pltpu.SMEM},
        vmem=20 << 20,
    )
    back = back.reshape(devices, per, 1, edges)
    got = lax.all_to_all(back, ("gx", "gz"), split_axis=0, concat_axis=0, tiled=True)
    block = shape((cx, cz, ny), F32)
    return tuple(
        call(
            backward_kernel,
            "backward",
            [block] * 4,
            square
            + [pltpu.VMEM((cells + edges, ny), BF16)] * 2
            + [pltpu.VMEM((edges, ny), F32)]
            + [pltpu.VMEM((cz, ny), F32)] * 2
            + planes
            + [pltpu.VMEM((cells, ny), F32)]
            + [pltpu.VMEM((cx, cz, ny), F32)] * 4
            + [pltpu.SemaphoreType.DMA((4,)), pltpu.SemaphoreType.DMA((ny // TILE,))]
            + [pltpu.SemaphoreType.DMA((3, cx))],
            6 * cells * ny * (ny + cells + edges),
            u_vel, v_vel, w_vel, u_low, u_high, w_low, w_high, got.reshape(ny, edges), modes,
            *tables, f32(to_cells), along_z, *halves(local.T), mux, mum,
            places={i: pl.ANY for i in (0, 1, 2, 8)},
            out_places={i: pl.ANY for i in range(4)},
            vmem=60 << 20,
        )
    )


def solution(mesh):
    spec = P("gx", "gz", None)
    return jax.shard_map(
        on_device, mesh=mesh, in_specs=(spec,) * 3, out_specs=(spec,) * 4, check_vma=False
    )
```
